512 devices in a mesh: chan: 4 (over x), filt: 32 (over z_hi, y, core), space: 4 (over z_lo).
Axes of the slice: x: 4, y: 4, z: 16 (z_hi: 4, z_lo: 4; z = z_hi * 4 + z_lo), core: 2. Of those that a mesh axis runs over, the one named last changes fastest.
Arguments:
- activations: bfloat16 [32, 32, 32, 512], P('filt', 'space', None, 'chan'), may hold values from -6 to 6
- weight: bfloat16 [27, 512, 512], P(None, 'chan', 'space'), may hold values from -0.0546875 to 0.0546875
- output_grad: bfloat16 [32, 32, 32, 512], P('filt', 'space', None, 'chan'), may hold values from -6 to 6
Outputs:
- output: bfloat16 [32, 32, 32, 512], P('filt', 'space', None, 'chan')
- input_grad: bfloat16 [32, 32, 32, 512], P('filt', 'space', None, 'chan')
- weight_grad: float32 [27, 512, 512], P(None, 'chan', 'space')
The draws below stay inside these ranges and needn't reach their ends.
All inputs are finite; a program needn't handle non-finite values.
Results may differ from the reference program's by a relative error of at most 0.0011.
Values may be sent and summed in bfloat16 or wider, within the bound.
No kernel may reach another device: no remote copies, remote signals or barrier semaphores. Data moves between devices by JAX's collectives and lax.ppermute only.
A program may use at most 64 MiB of HBM per device.

```python
import math
import jax
import jax.numpy as jnp
from jax import lax

CI = 512
CO = 512
HGT = 32
WID = 32
NDEP = 32


def block_levels(rng, extent, split, smallest, high):
    def one(position, shards_of):
        heights = jax.random.uniform(jax.random.fold_in(jax.random.fold_in(rng, 6), position), (shards_of,), jnp.float32, smallest / len(split), high / len(split))
        return jnp.repeat(jnp.exp(heights), extent[position] // shards_of).reshape((-1,) + (1,) * (len(extent) - position - 1))

    gain = one(*split[0])
    for cut in split[1:]:
        gain = gain * one(*cut)
    return gain


def noise(key, dims, scale, most, cuts=(), dtype=jnp.bfloat16):
    factor_of = block_levels(key, dims, cuts, -0.22, 0.18) if cuts else 1.0
    values = jax.random.normal(key, dims, jnp.float32) * scale * factor_of
    return jnp.minimum(jnp.maximum(values, -most), most).astype(dtype)


def setup_inputs(seed: int = 0) -> dict:
    key_of = jax.random.split(jax.random.key(seed), 4)
    activations = noise(key_of[0], (WID, NDEP, HGT, CI), 1.0, 6.0, ((0, 32), (1, 4), (3, 4)))
    weight = noise(key_of[1], (27, CI, CO), (27 * CI) ** -0.5, 0.0546875, ((1, 4), (2, 4)))
    output_grad = noise(key_of[2], (WID, NDEP, HGT, CO), 1.0, 6.0, ((0, 32), (1, 4), (3, 4)))
    return {"activations": activations, "weight": weight, "output_grad": output_grad}


forward_specs = ('NWDHC', 'WDHIO', 'NWDHC')
backward_specs = ('NWDHC', 'WDHOI', 'NWDHC')

def correlate(data, kernel, specs):
    result = lax.conv_general_dilated(data[None], kernel, (1, 1, 1), ((1, 1), (1, 1), (1, 1)), dimension_numbers=specs, preferred_element_type=jnp.float32)
    return result[0]

def reference(activations, weight, output_grad):
    kernel = weight.reshape(3, 3, 3, CI, CO)
    output = correlate(activations, kernel, forward_specs).astype(jnp.bfloat16)
    flipped = jnp.flip(kernel, (0, 1, 2))
    input_grad = correlate(output_grad, flipped, backward_specs).astype(jnp.bfloat16)
    padded = jnp.pad(activations, ((1, 1), (1, 1), (1, 1), (0, 0)))
    flat_grad = output_grad.reshape(-1, CO)
    gathered = []
    for wide_off in range(3):
        for deep_off in range(3):
            for high_off in range(3):
                window = padded[wide_off:wide_off + WID, deep_off:deep_off + NDEP, high_off:high_off + HGT, :].reshape(-1, CI)
                gathered.append(jnp.dot(window.T, flat_grad, preferred_element_type=jnp.float32))
    weight_grad = jnp.stack(gathered) / math.sqrt(WID * NDEP * HGT)
    return (output, input_grad, weight_grad)
```

```python
import functools
import math

import jax
import jax.numpy as jnp
import numpy as np
from jax import lax
from jax.experimental import pallas as pl
from jax.experimental.pallas import tpu as pltpu
from jax.sharding import Mesh, PartitionSpec as P

AXES = ("chan", "zhi", "ring", "core", "space")
F32 = jnp.float32
BF16 = jnp.bfloat16
VMEM = pl.BlockSpec(memory_space=pltpu.VMEM)
SMEM = pl.BlockSpec(memory_space=pltpu.SMEM)


def permutation(sizes, move):
    pairs = []
    for source in range(math.prod(sizes)):
        target = move(*(int(v) for v in np.unravel_index(source, sizes)))
        if target is not None:
            pairs.append((source, int(np.ravel_multi_index(target, sizes))))
    return pairs


def column_move(sizes, step, swap):
    _, zhis, rings, cores, _ = sizes

    def move(chan, zhi, ring, core, space):
        column = (zhi * rings + ring) * cores + core + step
        if not 0 <= column < zhis * rings * cores:
            return None
        rest = (column // (rings * cores), column // cores % rings, column % cores)
        return (space, *rest, chan) if swap else (chan, *rest, space)

    return permutation(sizes, move)


def height_mask(rows, height, at):
    return lax.broadcasted_iota(jnp.int32, (rows, 128), 0) % height == at


def shifted(value, height, step):
    rows = value.shape[0]
    edge = 0 if step < 0 else height - 1
    rolled = pltpu.roll(value, (-step) % rows, 0)
    return jnp.where(height_mask(rows, height, edge), 0.0, rolled)


def fill_padded(padded, block):
    columns, planes, height, lanes = block.shape
    zero = jnp.zeros((columns, 1, height, lanes), BF16)
    padded[:, 0:1] = zero
    padded[:, planes + 1 : planes + 2] = zero
    padded[:, 1 : planes + 1] = block[...]


def conv_kernel(backward, block, weight, out, padded, flat):
    slabs, rows, lanes = out.shape
    height = block.shape[2]
    planes = rows // height
    fill_padded(padded, block)
    for cell in range(9):
        for r in range(3):
            if backward:
                flat[r * lanes : (r + 1) * lanes, cell * lanes : (cell + 1) * lanes] = weight[3 * cell + r]
            else:
                flat[cell * lanes : (cell + 1) * lanes, r * lanes : (r + 1) * lanes] = weight[3 * cell + r]
    for slab in range(slabs):
        pieces = []
        for p in range(3):
            for q in range(3):
                column, plane = (2 - p, 2 - q) if backward else (p, q)
                start = slab * planes + plane
                pieces.append(padded[column, start : start + planes].reshape(rows, lanes))
        lhs = jnp.concatenate(pieces, axis=1)
        dims = (((1,), (1 if backward else 0,)), ((), ()))
        taps = lax.dot_general(lhs, flat[...], dims, preferred_element_type=F32)
        low, high = (2, 0) if backward else (0, 2)
        total = taps[:, lanes : 2 * lanes]
        total += shifted(taps[:, low * lanes : (low + 1) * lanes], height, -1)
        total += shifted(taps[:, high * lanes : (high + 1) * lanes], height, 1)
        out[slab] = total


def convolve(backward, block, weight, slabs):
    columns, planes, height, lanes = block.shape
    rows = planes * height
    flat = (3 * lanes, 9 * lanes) if backward else (9 * lanes, 3 * lanes)
    return pl.pallas_call(
        functools.partial(conv_kernel, backward),
        out_shape=jax.ShapeDtypeStruct((slabs, rows // slabs, lanes), F32),
        in_specs=[VMEM, VMEM],
        out_specs=VMEM,
        scratch_shapes=[
            pltpu.VMEM((columns, planes + 2, height, lanes), BF16),
            pltpu.VMEM(flat, BF16),
        ],
        compiler_params=pltpu.CompilerParams(vmem_limit_bytes=40 << 20),
        cost_estimate=pl.CostEstimate(
            flops=2 * 27 * rows * lanes * lanes, bytes_accessed=3 << 20, transcendentals=0
        ),
        name="input_grad" if backward else "forward",
    )(block, weight)


def filter_kernel(core, data, grad, keep, send, padded, turned, taps):
    planes, height, lanes = data.shape
    rows = planes * height
    fill_padded(padded, grad)
    flat = data[...].reshape(rows, lanes).astype(F32)
    turned[0:lanes] = shifted(flat, height, -1).T.astype(BF16)
    turned[lanes : 2 * lanes] = flat.T.astype(BF16)
    turned[2 * lanes : 3 * lanes] = shifted(flat, height, 1).T.astype(BF16)
    for p in range(3):
        pieces = [padded[2 - p, 2 - q : 2 - q + planes].reshape(rows, lanes) for q in range(3)]
        rhs = jnp.concatenate(pieces, axis=1)
        result = jnp.dot(turned[...], rhs, preferred_element_type=F32)
        for q in range(3):
            for r in range(3):
                tap = 9 * p + 3 * q + r
                taps[tap * lanes : (tap + 1) * lanes] = result[
                    r * lanes : (r + 1) * lanes, q * lanes : (q + 1) * lanes
                ]
    taps[27 * lanes :] = jnp.zeros((lanes, lanes), F32)
    half = keep.shape[0]

    @pl.when(core[0] == 0)
    def _():
        keep[...] = taps[0:half]
        send[...] = taps[half : 2 * half]

    @pl.when(core[0] == 1)
    def _():
        keep[...] = taps[half : 2 * half]
        send[...] = taps[0:half]


def filter_partial(data, grad, core):
    planes, height, lanes = data.shape
    rows = planes * height
    half = jax.ShapeDtypeStruct((14 * lanes, lanes), F32)
    return pl.pallas_call(
        filter_kernel,
        out_shape=(half, half),
        in_specs=[SMEM, VMEM, VMEM],
        out_specs=(VMEM, VMEM),
        scratch_shapes=[
            pltpu.VMEM((3, planes + 2, height, lanes), BF16),
            pltpu.VMEM((3 * lanes, rows), BF16),
            pltpu.VMEM((28 * lanes, lanes), F32),
        ],
        compiler_params=pltpu.CompilerParams(vmem_limit_bytes=40 << 20),
        cost_estimate=pl.CostEstimate(
            flops=2 * 27 * rows * lanes * lanes, bytes_accessed=3 << 20, transcendentals=0
        ),
        name="filter_grad",
    )(core, data, grad)


def exchange(block, axis):
    return lax.all_to_all(block, axis, split_axis=0, concat_axis=0, tiled=True)


def shards(sizes, activations, weight, output_grad):
    _, zhis, rings, cores, spaces = sizes
    act_low = lax.ppermute(activations, AXES, column_move(sizes, 1, False))
    act_high = lax.ppermute(activations, AXES, column_move(sizes, -1, False))
    grad_low = lax.ppermute(output_grad, AXES, column_move(sizes, 1, True))
    grad_mid = lax.ppermute(output_grad, AXES, column_move(sizes, 0, True))
    grad_high = lax.ppermute(output_grad, AXES, column_move(sizes, -1, True))
    grad = jnp.concatenate([grad_low, grad_mid, grad_high], axis=0)
    grad = lax.all_gather(grad, "chan", axis=1, tiled=True)
    data = jnp.concatenate([act_low, activations, act_high], axis=0)
    data = lax.all_gather(data, "space", axis=1, tiled=True)
    lanes = activations.shape[3]
    core = lax.axis_index("core").reshape(1)

    keep, send = filter_partial(data[1], grad, core)
    half = keep + lax.ppermute(send, "core", [(0, 1), (1, 0)])
    quarter = exchange(half.reshape(rings, -1, lanes), "ring").sum(0)
    part = exchange(quarter.reshape(zhis, -1, lanes), "zhi").sum(0)
    cell_count = sizes[1] * rings * cores * grad.shape[1] * grad.shape[2]
    part = part / math.sqrt(cell_count)
    quarter = lax.all_gather(part, "zhi", axis=0, tiled=True)
    half = lax.all_gather(quarter, "ring", axis=0, tiled=True)
    other = lax.ppermute(half, "core", [(0, 1), (1, 0)])
    first = core[0] == 0
    low = jnp.where(first, half, other)
    high = jnp.where(first, other, half)
    taps = weight.shape[0]
    filter_grad = jnp.concatenate([low, high[: taps * lanes - low.shape[0]]], axis=0)
    filter_grad = filter_grad.reshape(weight.shape)

    forward = exchange(convolve(False, data, weight, spaces), "chan").sum(0).astype(BF16)
    output = lax.ppermute(forward, AXES, column_move(sizes, 0, True)).reshape(activations.shape)
    back = exchange(convolve(True, grad, weight, spaces), "space").sum(0).astype(BF16)
    input_grad = back.reshape(activations.shape)
    return output, input_grad, filter_grad


def solution(mesh):
    chans, filts, spaces = (mesh.shape[name] for name in ("chan", "filt", "space"))
    sizes = (chans, filts // 8, 4, 2, spaces)
    fine = Mesh(mesh.devices.reshape(sizes), AXES)
    cells = P(("zhi", "ring", "core"), "space", None, "chan")
    filters = P(None, "chan", "space")
    return jax.shard_map(
        functools.partial(shards, sizes),
        mesh=fine,
        in_specs=(cells, filters, cells),
        out_specs=(cells, cells, filters),
        check_vma=False,
    )
```

```python
import functools
import math

import jax
import jax.numpy as jnp
import numpy as np
from jax import lax
from jax.experimental import pallas as pl
from jax.experimental.pallas import tpu as pltpu
from jax.sharding import Mesh, PartitionSpec as P

AXES = ("chan", "zhi", "ring", "core", "space")
F32 = jnp.float32
BF16 = jnp.bfloat16
VMEM = pl.BlockSpec(memory_space=pltpu.VMEM)
SMEM = pl.BlockSpec(memory_space=pltpu.SMEM)


def permutation(sizes, move):
    pairs = []
    for source in range(math.prod(sizes)):
        target = move(*(int(v) for v in np.unravel_index(source, sizes)))
        if target is not None:
            pairs.append((source, int(np.ravel_multi_index(target, sizes))))
    return pairs


def column_move(sizes, step, swap):
    _, zhis, rings, cores, _ = sizes

    def move(chan, zhi, ring, core, space):
        column = (zhi * rings + ring) * cores + core + step
        if not 0 <= column < zhis * rings * cores:
            return None
        rest = (column // (rings * cores), column // cores % rings, column % cores)
        return (space, *rest, chan) if swap else (chan, *rest, space)

    return permutation(sizes, move)


def height_mask(rows, height, at):
    return lax.broadcasted_iota(jnp.int32, (rows, 128), 0) % height == at


def shifted(value, height, step):
    rows = value.shape[0]
    edge = 0 if step < 0 else height - 1
    rolled = pltpu.roll(value, (-step) % rows, 0)
    return jnp.where(height_mask(rows, height, edge), 0.0, rolled)


def fill_padded(padded, block):
    columns, planes, height, lanes = block.shape
    zero = jnp.zeros((columns, 1, height, lanes), BF16)
    padded[:, 0:1] = zero
    padded[:, planes + 1 : planes + 2] = zero
    padded[:, 1 : planes + 1] = block[...]


def conv_kernel(backward, block, weight, out, padded, flat):
    slabs, rows, lanes = out.shape
    height = block.shape[2]
    planes = rows // height
    fill_padded(padded, block)
    for cell in range(9):
        for r in range(3):
            if backward:
                flat[r * lanes : (r + 1) * lanes, cell * lanes : (cell + 1) * lanes] = weight[3 * cell + r]
            else:
                flat[cell * lanes : (cell + 1) * lanes, r * lanes : (r + 1) * lanes] = weight[3 * cell + r]
    for slab in range(slabs):
        pieces = []
        for p in range(3):
            for q in range(3):
                column, plane = (2 - p, 2 - q) if backward else (p, q)
                start = slab * planes + plane
                pieces.append(padded[column, start : start + planes].reshape(rows, lanes))
        lhs = jnp.concatenate(pieces, axis=1)
        dims = (((1,), (1 if backward else 0,)), ((), ()))
        taps = lax.dot_general(lhs, flat[...], dims, preferred_element_type=F32)
        low, high = (2, 0) if backward else (0, 2)
        total = taps[:, lanes : 2 * lanes]
        total += shifted(taps[:, low * lanes : (low + 1) * lanes], height, -1)
        total += shifted(taps[:, high * lanes : (high + 1) * lanes], height, 1)
        out[slab] = total


def convolve(backward, block, weight, slabs):
    columns, planes, height, lanes = block.shape
    rows = planes * height
    flat = (3 * lanes, 9 * lanes) if backward else (9 * lanes, 3 * lanes)
    return pl.pallas_call(
        functools.partial(conv_kernel, backward),
        out_shape=jax.ShapeDtypeStruct((slabs, rows // slabs, lanes), F32),
        in_specs=[VMEM, VMEM],
        out_specs=VMEM,
        scratch_shapes=[
            pltpu.VMEM((columns, planes + 2, height, lanes), BF16),
            pltpu.VMEM(flat, BF16),
        ],
        compiler_params=pltpu.CompilerParams(vmem_limit_bytes=40 << 20),
        cost_estimate=pl.CostEstimate(
            flops=2 * 27 * rows * lanes * lanes, bytes_accessed=3 << 20, transcendentals=0
        ),
        name="input_grad" if backward else "forward",
    )(block, weight)


def filter_kernel(core, data, grad, keep, send, padded, turned, taps):
    planes, height, lanes = data.shape
    rows = planes * height
    fill_padded(padded, grad)
    flat = data[...].reshape(rows, lanes).astype(F32)
    turned[0:lanes] = shifted(flat, height, -1).T.astype(BF16)
    turned[lanes : 2 * lanes] = flat.T.astype(BF16)
    turned[2 * lanes : 3 * lanes] = shifted(flat, height, 1).T.astype(BF16)
    for p in range(3):
        pieces = [padded[2 - p, 2 - q : 2 - q + planes].reshape(rows, lanes) for q in range(3)]
        rhs = jnp.concatenate(pieces, axis=1)
        result = jnp.dot(turned[...], rhs, preferred_element_type=F32)
        for q in range(3):
            for r in range(3):
                tap = 9 * p + 3 * q + r
                taps[tap * lanes : (tap + 1) * lanes] = result[
                    r * lanes : (r + 1) * lanes, q * lanes : (q + 1) * lanes
                ]
    taps[27 * lanes :] = jnp.zeros((lanes, lanes), F32)
    half = keep.shape[0]

    @pl.when(core[0] == 0)
    def _():
        keep[...] = taps[0:half]
        send[...] = taps[half : 2 * half]

    @pl.when(core[0] == 1)
    def _():
        keep[...] = taps[half : 2 * half]
        send[...] = taps[0:half]


def filter_partial(data, grad, core):
    planes, height, lanes = data.shape
    rows = planes * height
    half = jax.ShapeDtypeStruct((14 * lanes, lanes), F32)
    return pl.pallas_call(
        filter_kernel,
        out_shape=(half, half),
        in_specs=[SMEM, VMEM, VMEM],
        out_specs=(VMEM, VMEM),
        scratch_shapes=[
            pltpu.VMEM((3, planes + 2, height, lanes), BF16),
            pltpu.VMEM((3 * lanes, rows), BF16),
            pltpu.VMEM((28 * lanes, lanes), F32),
        ],
        compiler_params=pltpu.CompilerParams(vmem_limit_bytes=40 << 20),
        cost_estimate=pl.CostEstimate(
            flops=2 * 27 * rows * lanes * lanes, bytes_accessed=3 << 20, transcendentals=0
        ),
        name="filter_grad",
    )(core, data, grad)


def exchange(block, axis):
    return lax.all_to_all(block, axis, split_axis=0, concat_axis=0, tiled=True)


def gather(block, axis):
    count = lax.axis_size(axis)
    return exchange(jnp.broadcast_to(block[None], (count, *block.shape)), axis)


def after(value, *others):
    return lax.optimization_barrier((value, *others))[0]


def shards(sizes, activations, weight, output_grad):
    _, zhis, rings, cores, spaces = sizes
    planes, height, lanes = activations.shape[1:]
    core = lax.axis_index("core").reshape(1)
    swap = [(0, 1), (1, 0)]

    own = gather(activations[0], "space").reshape(-1, height, lanes)
    grads = [
        lax.ppermute(output_grad, AXES, column_move(sizes, step, True)) for step in (1, 0, -1)
    ]
    grad = lax.all_gather(jnp.concatenate(grads, axis=0), "chan", axis=1, tiled=True)

    keep, send = filter_partial(own, grad, core)
    moved = lax.ppermute(send, "core", swap)
    edge = after(activations, send)
    low = lax.ppermute(edge, AXES, column_move(sizes, 1, False))
    high = lax.ppermute(edge, AXES, column_move(sizes, -1, False))
    half = keep + moved
    half = after(half, low, high)

    moved = exchange(half.reshape(rings, -1, lanes), "ring")
    sides = jnp.concatenate([after(low, half), high], axis=0)
    sides = lax.all_gather(sides, "space", axis=1, tiled=True)
    quarter = moved.sum(0)
    quarter = after(quarter, sides)

    moved = exchange(quarter.reshape(zhis, -1, lanes), "zhi")
    data = jnp.stack([after(sides, quarter)[0], own, sides[1]], axis=0)
    forward = convolve(False, data, weight, spaces)
    back = convolve(True, after(grad, quarter), weight, spaces)
    forward = exchange(forward, "chan")
    cell_count = sizes[1] * rings * cores * grad.shape[1] * grad.shape[2]
    part = moved.sum(0) / math.sqrt(cell_count)
    part = after(part, back, forward)

    moved = gather(part, "zhi")
    forward = after(forward, part).sum(0).astype(BF16)
    output = lax.ppermute(forward, AXES, column_move(sizes, 0, True)).reshape(activations.shape)
    quarter = moved.reshape(-1, lanes)
    quarter = after(quarter, output)

    moved = gather(quarter, "ring")
    back = exchange(after(back, quarter), "space").sum(0).astype(BF16)
    input_grad = back.reshape(activations.shape)
    half = moved.reshape(-1, lanes)
    half = after(half, input_grad)

    other = lax.ppermute(half, "core", swap)
    first = core[0] == 0
    low = jnp.where(first, half, other)
    high = jnp.where(first, other, half)
    taps = weight.shape[0]
    filter_grad = jnp.concatenate([low, high[: taps * lanes - low.shape[0]]], axis=0)
    filter_grad = filter_grad.reshape(weight.shape)
    return output, input_grad, filter_grad


def solution(mesh):
    chans, filts, spaces = (mesh.shape[name] for name in ("chan", "filt", "space"))
    sizes = (chans, filts // 8, 4, 2, spaces)
    fine = Mesh(mesh.devices.reshape(sizes), AXES)
    cells = P(("zhi", "ring", "core"), "space", None, "chan")
    filters = P(None, "chan", "space")
    return jax.shard_map(
        functools.partial(shards, sizes),
        mesh=fine,
        in_specs=(cells, filters, cells),
        out_specs=(cells, cells, filters),
        check_vma=False,
    )
```

```python
import functools
import math

import jax
import jax.numpy as jnp
import numpy as np
from jax import lax
from jax.experimental import pallas as pl
from jax.experimental.pallas import tpu as pltpu
from jax.sharding import Mesh, PartitionSpec as P

AXES = ("chan", "zhi", "ring", "core", "space")
F32 = jnp.float32
BF16 = jnp.bfloat16
VMEM = pl.BlockSpec(memory_space=pltpu.VMEM)
SMEM = pl.BlockSpec(memory_space=pltpu.SMEM)


def permutation(sizes, move):
    pairs = []
    for source in range(math.prod(sizes)):
        target = move(*(int(v) for v in np.unravel_index(source, sizes)))
        if target is not None:
            pairs.append((source, int(np.ravel_multi_index(target, sizes))))
    return pairs


def column_move(sizes, step, swap):
    _, zhis, rings, cores, _ = sizes

    def move(chan, zhi, ring, core, space):
        column = (zhi * rings + ring) * cores + core + step
        if not 0 <= column < zhis * rings * cores:
            return None
        rest = (column // (rings * cores), column // cores % rings, column % cores)
        return (space, *rest, chan) if swap else (chan, *rest, space)

    return permutation(sizes, move)


def height_mask(rows, height, at):
    return lax.broadcasted_iota(jnp.int32, (rows, 128), 0) % height == at


def shifted(value, height, step):
    rows = value.shape[0]
    edge = 0 if step < 0 else height - 1
    rolled = pltpu.roll(value, (-step) % rows, 0)
    return jnp.where(height_mask(rows, height, edge), 0.0, rolled)


def fill_padded(padded, block):
    _, planes, height, lanes = block.shape
    columns = padded.shape[0]
    zero = jnp.zeros((columns, 1, height, lanes), BF16)
    padded[:, 0:1] = zero
    padded[:, planes + 1 : planes + 2] = zero
    padded[:, 1 : planes + 1] = block[0:columns]


def conv_kernel(backward, block, weight, out, padded, flat):
    slabs, rows, lanes = out.shape
    height = block.shape[2]
    planes = rows // height
    fill_padded(padded, block)
    for cell in range(9):
        for r in range(3):
            if backward:
                flat[r * lanes : (r + 1) * lanes, cell * lanes : (cell + 1) * lanes] = weight[3 * cell + r]
            else:
                flat[cell * lanes : (cell + 1) * lanes, r * lanes : (r + 1) * lanes] = weight[3 * cell + r]
    for slab in range(slabs):
        pieces = []
        for p in range(3):
            for q in range(3):
                column, plane = (2 - p, 2 - q) if backward else (p, q)
                start = slab * planes + plane
                pieces.append(padded[column, start : start + planes].reshape(rows, lanes))
        lhs = jnp.concatenate(pieces, axis=1)
        dims = (((1,), (1 if backward else 0,)), ((), ()))
        taps = lax.dot_general(lhs, flat[...], dims, preferred_element_type=F32)
        low, high = (2, 0) if backward else (0, 2)
        total = taps[:, lanes : 2 * lanes]
        total += shifted(taps[:, low * lanes : (low + 1) * lanes], height, -1)
        total += shifted(taps[:, high * lanes : (high + 1) * lanes], height, 1)
        out[slab] = total


def convolve(backward, block, weight, slabs):
    _, planes, height, lanes = block.shape
    rows = planes * height
    flat = (3 * lanes, 9 * lanes) if backward else (9 * lanes, 3 * lanes)
    return pl.pallas_call(
        functools.partial(conv_kernel, backward),
        out_shape=jax.ShapeDtypeStruct((slabs, rows // slabs, lanes), F32),
        in_specs=[VMEM, VMEM],
        out_specs=VMEM,
        scratch_shapes=[
            pltpu.VMEM((3, planes + 2, height, lanes), BF16),
            pltpu.VMEM(flat, BF16),
        ],
        compiler_params=pltpu.CompilerParams(vmem_limit_bytes=40 << 20),
        cost_estimate=pl.CostEstimate(
            flops=2 * 27 * rows * lanes * lanes, bytes_accessed=3 << 20, transcendentals=0
        ),
        name="input_grad" if backward else "forward",
    )(block, weight)


def filter_kernel(core, data, grad, keep, send, padded, turned, taps):
    planes, height, lanes = data.shape
    rows = planes * height
    fill_padded(padded, grad)
    flat = data[...].reshape(rows, lanes).astype(F32)
    turned[0:lanes] = shifted(flat, height, -1).T.astype(BF16)
    turned[lanes : 2 * lanes] = flat.T.astype(BF16)
    turned[2 * lanes : 3 * lanes] = shifted(flat, height, 1).T.astype(BF16)
    for p in range(3):
        pieces = [padded[2 - p, 2 - q : 2 - q + planes].reshape(rows, lanes) for q in range(3)]
        rhs = jnp.concatenate(pieces, axis=1)
        result = jnp.dot(turned[...], rhs, preferred_element_type=F32)
        for q in range(3):
            for r in range(3):
                tap = 9 * p + 3 * q + r
                taps[tap * lanes : (tap + 1) * lanes] = result[
                    r * lanes : (r + 1) * lanes, q * lanes : (q + 1) * lanes
                ]
    taps[27 * lanes :] = jnp.zeros((lanes, lanes), F32)
    half = keep.shape[0]

    @pl.when(core[0] == 0)
    def _():
        keep[...] = taps[0:half]
        send[...] = taps[half : 2 * half]

    @pl.when(core[0] == 1)
    def _():
        keep[...] = taps[half : 2 * half]
        send[...] = taps[0:half]


def filter_partial(data, grad, core):
    planes, height, lanes = data.shape
    rows = planes * height
    half = jax.ShapeDtypeStruct((14 * lanes, lanes), F32)
    return pl.pallas_call(
        filter_kernel,
        out_shape=(half, half),
        in_specs=[SMEM, VMEM, VMEM],
        out_specs=(VMEM, VMEM),
        scratch_shapes=[
            pltpu.VMEM((3, planes + 2, height, lanes), BF16),
            pltpu.VMEM((3 * lanes, rows), BF16),
            pltpu.VMEM((28 * lanes, lanes), F32),
        ],
        compiler_params=pltpu.CompilerParams(vmem_limit_bytes=40 << 20),
        cost_estimate=pl.CostEstimate(
            flops=2 * 27 * rows * lanes * lanes, bytes_accessed=3 << 20, transcendentals=0
        ),
        name="filter_grad",
    )(core, data, grad)


def exchange(block, axis):
    return lax.all_to_all(block, axis, split_axis=0, concat_axis=0, tiled=True)


def gather(block, axis):
    count = lax.axis_size(axis)
    return exchange(jnp.broadcast_to(block[None], (count, *block.shape)), axis)


def after(value, *others):
    return lax.optimization_barrier((value, *others))[0]


def shards(sizes, activations, weight, output_grad):
    _, zhis, rings, cores, spaces = sizes
    planes, height, lanes = activations.shape[1:]
    core = lax.axis_index("core").reshape(1)
    swap = [(0, 1), (1, 0)]

    own = gather(activations[0], "space").reshape(-1, height, lanes)
    grads = [
        lax.ppermute(output_grad, AXES, column_move(sizes, step, True)) for step in (1, 0, -1)
    ]
    low = lax.ppermute(activations, AXES, column_move(sizes, 1, False))
    high = lax.ppermute(activations, AXES, column_move(sizes, -1, False))
    sides = jnp.concatenate([low, activations, high, low], axis=0)
    data = lax.all_gather(sides, "space", axis=1, tiled=True)
    grad = after(jnp.concatenate(grads, axis=0), sides)
    grad = lax.all_gather(grad, "chan", axis=1, tiled=True)

    keep, send = filter_partial(own, grad, core)
    moved = lax.ppermute(send, "core", swap)
    back = convolve(True, after(grad, send), weight, spaces)
    half = after(keep + moved, back)
    back = lax.psum_scatter(back, "space", scatter_dimension=0, tiled=True)

    moved = exchange(half.reshape(rings, -1, lanes), "ring")
    quarter, data = lax.optimization_barrier((moved.sum(0), data))

    moved = exchange(quarter.reshape(zhis, -1, lanes), "zhi")
    forward = convolve(False, data, weight, spaces)
    cell_count = sizes[1] * rings * cores * grad.shape[1] * grad.shape[2]
    part = moved.sum(0) / math.sqrt(cell_count)
    part, back = lax.optimization_barrier((after(part, forward), back))
    forward = lax.psum_scatter(forward, "chan", scatter_dimension=0, tiled=True)

    quarter = gather(part, "zhi").reshape(-1, lanes)

    half = gather(quarter, "ring").reshape(-1, lanes)
    half, forward = lax.optimization_barrier((half, forward))
    forward = forward[0].astype(BF16)
    output = lax.ppermute(forward, AXES, column_move(sizes, 0, True)).reshape(activations.shape)
    input_grad = back[0].astype(BF16).reshape(activations.shape)

    other = lax.ppermute(half, "core", swap)
    first = core[0] == 0
    low = jnp.where(first, half, other)
    high = jnp.where(first, other, half)
    taps = weight.shape[0]
    filter_grad = jnp.concatenate([low, high[: taps * lanes - low.shape[0]]], axis=0)
    filter_grad = filter_grad.reshape(weight.shape)
    return output, input_grad, filter_grad


def solution(mesh):
    chans, filts, spaces = (mesh.shape[name] for name in ("chan", "filt", "space"))
    sizes = (chans, filts // 8, 4, 2, spaces)
    fine = Mesh(mesh.devices.reshape(sizes), AXES)
    cells = P(("zhi", "ring", "core"), "space", None, "chan")
    filters = P(None, "chan", "space")
    return jax.shard_map(
        functools.partial(shards, sizes),
        mesh=fine,
        in_specs=(cells, filters, cells),
        out_specs=(cells, cells, filters),
        check_vma=False,
    )
```

```python
import functools
import math

import jax
import jax.numpy as jnp
import numpy as np
from jax import lax
from jax.experimental import pallas as pl
from jax.experimental.pallas import tpu as pltpu
from jax.sharding import Mesh, PartitionSpec as P

AXES = ("chan", "zhi", "ring", "core", "space")
F32 = jnp.float32
BF16 = jnp.bfloat16
VMEM = pl.BlockSpec(memory_space=pltpu.VMEM)
SMEM = pl.BlockSpec(memory_space=pltpu.SMEM)


def permutation(sizes, move):
    pairs = []
    for source in range(math.prod(sizes)):
        target = move(*(int(v) for v in np.unravel_index(source, sizes)))
        if target is not None:
            pairs.append((source, int(np.ravel_multi_index(target, sizes))))
    return pairs


def column_move(sizes, step, swap):
    _, zhis, rings, cores, _ = sizes

    def move(chan, zhi, ring, core, space):
        column = (zhi * rings + ring) * cores + core + step
        if not 0 <= column < zhis * rings * cores:
            return None
        rest = (column // (rings * cores), column // cores % rings, column % cores)
        return (space, *rest, chan) if swap else (chan, *rest, space)

    return permutation(sizes, move)


def height_mask(rows, height, at):
    return lax.broadcasted_iota(jnp.int32, (rows, 128), 0) % height == at


def shifted(value, height, step):
    rows = value.shape[0]
    edge = 0 if step < 0 else height - 1
    rolled = pltpu.roll(value, (-step) % rows, 0)
    return jnp.where(height_mask(rows, height, edge), 0.0, rolled)


def fill_padded(padded, block):
    columns, planes, height, lanes = padded.shape
    planes -= 2
    zero = jnp.zeros((columns, 1, height, lanes), BF16)
    padded[:, 0:1] = zero
    padded[:, planes + 1 : planes + 2] = zero
    if len(block.shape) == 4:
        padded[:, 1 : planes + 1] = block[...]
    else:
        slabs, _, depth = block.shape[:3]
        for slab in range(slabs):
            padded[:, 1 + slab * depth : 1 + (slab + 1) * depth] = block[slab]


def conv_kernel(backward, me, block, weight, *refs):
    *outs, padded, flat = refs
    slabs = len(outs)
    rows, lanes = outs[0].shape
    height = block.shape[-2]
    planes = rows // height
    fill_padded(padded, block)
    for cell in range(9):
        for r in range(3):
            if backward:
                flat[r * lanes : (r + 1) * lanes, cell * lanes : (cell + 1) * lanes] = weight[3 * cell + r]
            else:
                flat[cell * lanes : (cell + 1) * lanes, r * lanes : (r + 1) * lanes] = weight[3 * cell + r]
    for step, out in enumerate(outs):
        slab = lax.rem(me[0] + step, slabs)
        pieces = []
        for p in range(3):
            for q in range(3):
                column, plane = (2 - p, 2 - q) if backward else (p, q)
                start = slab * planes + plane
                pieces.append(padded[column, pl.ds(start, planes)].reshape(rows, lanes))
        lhs = jnp.concatenate(pieces, axis=1)
        dims = (((1,), (1 if backward else 0,)), ((), ()))
        taps = lax.dot_general(lhs, flat[...], dims, preferred_element_type=F32)
        low, high = (2, 0) if backward else (0, 2)
        total = taps[:, lanes : 2 * lanes]
        total += shifted(taps[:, low * lanes : (low + 1) * lanes], height, -1)
        total += shifted(taps[:, high * lanes : (high + 1) * lanes], height, 1)
        out[...] = total


def convolve(backward, block, weight, slabs, me):
    height, lanes = block.shape[-2:]
    rows = block.size // (3 * lanes)
    planes = rows // height
    flat = (3 * lanes, 9 * lanes) if backward else (9 * lanes, 3 * lanes)
    return pl.pallas_call(
        functools.partial(conv_kernel, backward),
        out_shape=[jax.ShapeDtypeStruct((rows // slabs, lanes), F32)] * slabs,
        in_specs=[SMEM, VMEM, VMEM],
        out_specs=[VMEM] * slabs,
        scratch_shapes=[
            pltpu.VMEM((3, planes + 2, height, lanes), BF16),
            pltpu.VMEM(flat, BF16),
        ],
        compiler_params=pltpu.CompilerParams(vmem_limit_bytes=14 << 20),
        cost_estimate=pl.CostEstimate(
            flops=2 * 27 * rows * lanes * lanes, bytes_accessed=3 << 20, transcendentals=0
        ),
        name="input_grad" if backward else "forward",
    )(me, block, weight)


def filter_kernel(core, data, grad, keep, send, padded, turned, taps):
    planes, height, lanes = grad.shape[1:]
    rows = planes * height
    fill_padded(padded, grad)
    flat = data[:, 1].reshape(rows, lanes).astype(F32)
    turned[0:lanes] = shifted(flat, height, -1).T.astype(BF16)
    turned[lanes : 2 * lanes] = flat.T.astype(BF16)
    turned[2 * lanes : 3 * lanes] = shifted(flat, height, 1).T.astype(BF16)
    for p in range(3):
        pieces = [padded[2 - p, 2 - q : 2 - q + planes].reshape(rows, lanes) for q in range(3)]
        rhs = jnp.concatenate(pieces, axis=1)
        result = jnp.dot(turned[...], rhs, preferred_element_type=F32)
        for q in range(3):
            for r in range(3):
                tap = 9 * p + 3 * q + r
                taps[tap * lanes : (tap + 1) * lanes] = result[
                    r * lanes : (r + 1) * lanes, q * lanes : (q + 1) * lanes
                ]
    taps[27 * lanes :] = jnp.zeros((lanes, lanes), F32)
    half = keep.shape[0]

    @pl.when(core[0] == 0)
    def _():
        keep[...] = taps[0:half]
        send[...] = taps[half : 2 * half]

    @pl.when(core[0] == 1)
    def _():
        keep[...] = taps[half : 2 * half]
        send[...] = taps[0:half]


def filter_partial(data, grad, core):
    planes, height, lanes = grad.shape[1:]
    rows = planes * height
    half = jax.ShapeDtypeStruct((14 * lanes, lanes), F32)
    return pl.pallas_call(
        filter_kernel,
        out_shape=(half, half),
        in_specs=[SMEM, VMEM, VMEM],
        out_specs=(VMEM, VMEM),
        scratch_shapes=[
            pltpu.VMEM((3, planes + 2, height, lanes), BF16),
            pltpu.VMEM((3 * lanes, rows), BF16),
            pltpu.VMEM((28 * lanes, lanes), F32),
        ],
        compiler_params=pltpu.CompilerParams(vmem_limit_bytes=14 << 20),
        cost_estimate=pl.CostEstimate(
            flops=2 * 27 * rows * lanes * lanes, bytes_accessed=3 << 20, transcendentals=0
        ),
        name="filter_grad",
    )(core, data, grad)


def exchange(block, axis):
    return lax.all_to_all(block, axis, split_axis=0, concat_axis=0, tiled=True)


def gather(block, axis):
    count = lax.axis_size(axis)
    return exchange(jnp.broadcast_to(block[None], (count, *block.shape)), axis)


def reduced(blocks, axis):
    count = len(blocks)
    total = blocks[0]
    for step in range(1, count):
        total += lax.ppermute(blocks[step], axis, [(i, (i + step) % count) for i in range(count)])
    return total


def after(value, *others):
    return lax.optimization_barrier((value, *others))[0]


def shards(sizes, activations, weight, output_grad):
    _, zhis, rings, cores, spaces = sizes
    planes, height, lanes = activations.shape[1:]
    core = lax.axis_index("core").reshape(1)
    swap = [(0, 1), (1, 0)]

    low = lax.ppermute(activations, AXES, column_move(sizes, 1, False))
    high = lax.ppermute(activations, AXES, column_move(sizes, -1, False))
    sides = jnp.concatenate([low, activations, high], axis=0)
    data = gather(sides, "space")
    cotangent = after(output_grad, sides)
    grads = [lax.ppermute(cotangent, AXES, column_move(sizes, step, True)) for step in (1, 0, -1)]
    grad = jnp.concatenate(grads, axis=0)
    grad = lax.all_gather(grad, "chan", axis=1, tiled=True)

    keep, send = filter_partial(data, grad, core)
    moved = lax.ppermute(send, "core", swap)
    me = lax.axis_index("space").reshape(1)
    back = convolve(True, after(grad, send), weight, spaces, me)
    half, *back = lax.optimization_barrier((keep + moved, *back))

    moved = exchange(half.reshape(rings, -1, lanes), "ring")
    input_grad = reduced(back, "space").astype(BF16).reshape(activations.shape)
    quarter, input_grad = lax.optimization_barrier((moved.sum(0), input_grad))

    moved = exchange(quarter.reshape(zhis, -1, lanes), "zhi")
    me = lax.axis_index("chan").reshape(1)
    forward = convolve(False, after(data, quarter), weight, spaces, me)
    forward = reduced(forward, "chan").astype(BF16)
    cell_count = sizes[1] * rings * cores * grad.shape[1] * grad.shape[2]
    part = moved.sum(0) / math.sqrt(cell_count)
    part, forward = lax.optimization_barrier((part, forward))

    quarter = gather(part, "zhi").reshape(-1, lanes)
    output = lax.ppermute(forward, AXES, column_move(sizes, 0, True)).reshape(activations.shape)
    quarter, output = lax.optimization_barrier((quarter, output))

    half = gather(quarter, "ring").reshape(-1, lanes)

    other = lax.ppermute(half, "core", swap)
    first = core[0] == 0
    low = jnp.where(first, half, other)
    high = jnp.where(first, other, half)
    taps = weight.shape[0]
    filter_grad = jnp.concatenate([low, high[: taps * lanes - low.shape[0]]], axis=0)
    filter_grad = filter_grad.reshape(weight.shape)
    return output, input_grad, filter_grad


def solution(mesh):
    chans, filts, spaces = (mesh.shape[name] for name in ("chan", "filt", "space"))
    sizes = (chans, filts // 8, 4, 2, spaces)
    fine = Mesh(mesh.devices.reshape(sizes), AXES)
    cells = P(("zhi", "ring", "core"), "space", None, "chan")
    filters = P(None, "chan", "space")
    return jax.shard_map(
        functools.partial(shards, sizes),
        mesh=fine,
        in_specs=(cells, filters, cells),
        out_specs=(cells, cells, filters),
        check_vma=False,
    )
```

```python
import functools
import math

import jax
import jax.numpy as jnp
import numpy as np
from jax import lax
from jax.experimental import pallas as pl
from jax.experimental.pallas import tpu as pltpu
from jax.sharding import Mesh, PartitionSpec as P

AXES = ("chan", "zhi", "ring", "core", "space")
F32 = jnp.float32
BF16 = jnp.bfloat16
VMEM = pl.BlockSpec(memory_space=pltpu.VMEM)
SMEM = pl.BlockSpec(memory_space=pltpu.SMEM)


def permutation(sizes, move):
    pairs = []
    for source in range(math.prod(sizes)):
        target = move(*(int(v) for v in np.unravel_index(source, sizes)))
        if target is not None:
            pairs.append((source, int(np.ravel_multi_index(target, sizes))))
    return pairs


def outer_neighbour(sizes):
    _, zhis, rings, cores, _ = sizes

    def move(chan, zhi, ring, core, space):
        column = (zhi * rings + ring) * cores + core
        column += 1 if column % 2 else -1
        if not 0 <= column < zhis * rings * cores:
            return None
        return (chan, column // (rings * cores), column // cores % rings, column % cores, space)

    return permutation(sizes, move)


def transposed(sizes):
    return permutation(sizes, lambda chan, zhi, ring, core, space: (space, zhi, ring, core, chan))


def height_mask(rows, height, at):
    return lax.broadcasted_iota(jnp.int32, (rows, 128), 0) % height == at


def shifted(value, height, step):
    rows = value.shape[0]
    edge = 0 if step < 0 else height - 1
    rolled = pltpu.roll(value, (-step) % rows, 0)
    return jnp.where(height_mask(rows, height, edge), 0.0, rolled)


def fill_padded(padded, block, core):
    columns, planes, height, lanes = padded.shape
    planes -= 2
    zero = jnp.zeros((columns, 1, height, lanes), BF16)
    padded[:, 0:1] = zero
    padded[:, planes + 1 : planes + 2] = zero
    low = 2 - core
    for column, source in enumerate((low, 0, 3 - low)):
        if len(block.shape) == 4:
            padded[column, 1 : planes + 1] = block[source]
        else:
            slabs, _, depth = block.shape[:3]
            for slab in range(slabs):
                padded[column, 1 + slab * depth : 1 + (slab + 1) * depth] = block[slab, source]


def conv_kernel(backward, core, block, weight, out, padded, flat):
    slabs, rows, lanes = out.shape
    height = block.shape[-2]
    planes = rows // height
    fill_padded(padded, block, core[0])
    for cell in range(9):
        for r in range(3):
            if backward:
                flat[r * lanes : (r + 1) * lanes, cell * lanes : (cell + 1) * lanes] = weight[3 * cell + r]
            else:
                flat[cell * lanes : (cell + 1) * lanes, r * lanes : (r + 1) * lanes] = weight[3 * cell + r]
    for slab in range(slabs):
        pieces = []
        for p in range(3):
            for q in range(3):
                column, plane = (2 - p, 2 - q) if backward else (p, q)
                start = slab * planes + plane
                pieces.append(padded[column, start : start + planes].reshape(rows, lanes))
        lhs = jnp.concatenate(pieces, axis=1)
        dims = (((1,), (1 if backward else 0,)), ((), ()))
        taps = lax.dot_general(lhs, flat[...], dims, preferred_element_type=F32)
        low, high = (2, 0) if backward else (0, 2)
        total = taps[:, lanes : 2 * lanes]
        total += shifted(taps[:, low * lanes : (low + 1) * lanes], height, -1)
        total += shifted(taps[:, high * lanes : (high + 1) * lanes], height, 1)
        out[slab] = total


def convolve(backward, core, block, weight, slabs):
    height, lanes = block.shape[-2:]
    rows = block.size // (3 * lanes)
    planes = rows // height
    flat = (3 * lanes, 9 * lanes) if backward else (9 * lanes, 3 * lanes)
    return pl.pallas_call(
        functools.partial(conv_kernel, backward),
        out_shape=jax.ShapeDtypeStruct((slabs, rows // slabs, lanes), F32),
        in_specs=[SMEM, VMEM, VMEM],
        out_specs=VMEM,
        scratch_shapes=[
            pltpu.VMEM((3, planes + 2, height, lanes), BF16),
            pltpu.VMEM(flat, BF16),
        ],
        compiler_params=pltpu.CompilerParams(vmem_limit_bytes=14 << 20),
        cost_estimate=pl.CostEstimate(
            flops=2 * 27 * rows * lanes * lanes, bytes_accessed=3 << 20, transcendentals=0
        ),
        name="input_grad" if backward else "forward",
    )(core, block, weight)


def filter_kernel(core, data, grad, keep, send, padded, turned, taps):
    planes, height, lanes = grad.shape[1:]
    rows = planes * height
    fill_padded(padded, grad, core[0])
    flat = data[:, 0].reshape(rows, lanes).astype(F32)
    turned[0:lanes] = shifted(flat, height, -1).T.astype(BF16)
    turned[lanes : 2 * lanes] = flat.T.astype(BF16)
    turned[2 * lanes : 3 * lanes] = shifted(flat, height, 1).T.astype(BF16)
    for p in range(3):
        pieces = [padded[2 - p, 2 - q : 2 - q + planes].reshape(rows, lanes) for q in range(3)]
        rhs = jnp.concatenate(pieces, axis=1)
        result = jnp.dot(turned[...], rhs, preferred_element_type=F32)
        for q in range(3):
            for r in range(3):
                tap = 9 * p + 3 * q + r
                taps[tap * lanes : (tap + 1) * lanes] = result[
                    r * lanes : (r + 1) * lanes, q * lanes : (q + 1) * lanes
                ]
    taps[27 * lanes :] = jnp.zeros((lanes, lanes), F32)
    half = keep.shape[0]

    @pl.when(core[0] == 0)
    def _():
        keep[...] = taps[0:half]
        send[...] = taps[half : 2 * half]

    @pl.when(core[0] == 1)
    def _():
        keep[...] = taps[half : 2 * half]
        send[...] = taps[0:half]


def filter_partial(data, grad, core):
    planes, height, lanes = grad.shape[1:]
    rows = planes * height
    half = jax.ShapeDtypeStruct((14 * lanes, lanes), F32)
    return pl.pallas_call(
        filter_kernel,
        out_shape=(half, half),
        in_specs=[SMEM, VMEM, VMEM],
        out_specs=(VMEM, VMEM),
        scratch_shapes=[
            pltpu.VMEM((3, planes + 2, height, lanes), BF16),
            pltpu.VMEM((3 * lanes, rows), BF16),
            pltpu.VMEM((28 * lanes, lanes), F32),
        ],
        compiler_params=pltpu.CompilerParams(vmem_limit_bytes=14 << 20),
        cost_estimate=pl.CostEstimate(
            flops=2 * 27 * rows * lanes * lanes, bytes_accessed=3 << 20, transcendentals=0
        ),
        name="filter_grad",
    )(core, data, grad)


def exchange(block, axis):
    return lax.all_to_all(block, axis, split_axis=0, concat_axis=0, tiled=True)


def gather(block, axis):
    count = lax.axis_size(axis)
    return exchange(jnp.broadcast_to(block[None], (count, *block.shape)), axis)


def after(value, *others):
    return lax.optimization_barrier((value, *others))[0]


def shards(sizes, activations, weight, output_grad):
    _, zhis, rings, cores, spaces = sizes
    planes, height, lanes = activations.shape[1:]
    core = lax.axis_index("core").reshape(1)
    swap = [(0, 1), (1, 0)]

    both = jnp.concatenate([activations, output_grad], axis=0)
    inner = lax.ppermute(both, "core", swap)
    outer = lax.ppermute(both, AXES, outer_neighbour(sizes))
    data = gather(jnp.concatenate([activations, inner[:1], outer[:1]], axis=0), "space")
    grad = jnp.concatenate([output_grad, inner[1:], outer[1:]], axis=0)
    grad = lax.ppermute(grad, AXES, transposed(sizes))
    grad = lax.all_gather(grad, "chan", axis=1, tiled=True)

    keep, send = filter_partial(data, grad, core)
    moved = lax.ppermute(send, "core", swap)
    back = convolve(True, core, after(grad, send), weight, spaces)
    forward = convolve(False, core, after(data, back), weight, spaces)
    half, back, forward = lax.optimization_barrier((keep + moved, back, forward))
    back = lax.psum_scatter(back, "space", scatter_dimension=0, tiled=True)
    forward = lax.psum_scatter(forward, "chan", scatter_dimension=0, tiled=True)

    quarter = exchange(half.reshape(rings, -1, lanes), "ring").sum(0)
    part = exchange(quarter.reshape(zhis, -1, lanes), "zhi").sum(0)
    cell_count = sizes[1] * rings * cores * grad.shape[1] * grad.shape[2]
    part = part / math.sqrt(cell_count)
    part, forward = lax.optimization_barrier((part, forward))

    quarter = gather(part, "zhi").reshape(-1, lanes)
    output = lax.ppermute(forward[0].astype(BF16), AXES, transposed(sizes))
    output = output.reshape(activations.shape)
    quarter, back, output = lax.optimization_barrier((quarter, back, output))
    input_grad = back[0].astype(BF16).reshape(activations.shape)
    half = gather(quarter, "ring").reshape(-1, lanes)

    other = lax.ppermute(half, "core", swap)
    first = core[0] == 0
    low = jnp.where(first, half, other)
    high = jnp.where(first, other, half)
    taps = weight.shape[0]
    filter_grad = jnp.concatenate([low, high[: taps * lanes - low.shape[0]]], axis=0)
    filter_grad = filter_grad.reshape(weight.shape)
    return output, input_grad, filter_grad


def solution(mesh):
    chans, filts, spaces = (mesh.shape[name] for name in ("chan", "filt", "space"))
    sizes = (chans, filts // 8, 4, 2, spaces)
    fine = Mesh(mesh.devices.reshape(sizes), AXES)
    cells = P(("zhi", "ring", "core"), "space", None, "chan")
    filters = P(None, "chan", "space")
    return jax.shard_map(
        functools.partial(shards, sizes),
        mesh=fine,
        in_specs=(cells, filters, cells),
        out_specs=(cells, cells, filters),
        check_vma=False,
    )
```

```python
import functools
import math

import jax
import jax.numpy as jnp
import numpy as np
from jax import lax
from jax.experimental import pallas as pl
from jax.experimental.pallas import tpu as pltpu
from jax.sharding import Mesh, PartitionSpec as P

AXES = ("chan", "zhi", "ring", "core", "space")
F32 = jnp.float32
BF16 = jnp.bfloat16
VMEM = pl.BlockSpec(memory_space=pltpu.VMEM)
SMEM = pl.BlockSpec(memory_space=pltpu.SMEM)


def permutation(sizes, move):
    pairs = []
    for source in range(math.prod(sizes)):
        target = move(*(int(v) for v in np.unravel_index(source, sizes)))
        if target is not None:
            pairs.append((source, int(np.ravel_multi_index(target, sizes))))
    return pairs


def outer_neighbour(sizes):
    _, zhis, rings, cores, _ = sizes

    def move(chan, zhi, ring, core, space):
        column = (zhi * rings + ring) * cores + core
        column += 1 if column % 2 else -1
        if not 0 <= column < zhis * rings * cores:
            return None
        return (chan, column // (rings * cores), column // cores % rings, column % cores, space)

    return permutation(sizes, move)


def transposed(sizes):
    return permutation(sizes, lambda chan, zhi, ring, core, space: (space, zhi, ring, core, chan))


def height_mask(rows, height, at):
    return lax.broadcasted_iota(jnp.int32, (rows, 128), 0) % height == at


def shifted(value, height, step):
    rows = value.shape[0]
    edge = 0 if step < 0 else height - 1
    rolled = pltpu.roll(value, (-step) % rows, 0)
    return jnp.where(height_mask(rows, height, edge), 0.0, rolled)


def fill_padded(padded, pair, inner, core):
    planes, height, lanes = padded.shape[1:]
    planes -= 2
    zero = jnp.zeros((3, 1, height, lanes), BF16)
    padded[:, 0:1] = zero
    padded[:, planes + 1 : planes + 2] = zero
    for column, source in ((1, 0), (2 * core, 1)):
        if len(pair.shape) == 4:
            padded[column, 1 : planes + 1] = pair[source]
        else:
            slabs, _, depth = pair.shape[:3]
            for slab in range(slabs):
                padded[column, 1 + slab * depth : 1 + (slab + 1) * depth] = pair[slab, source]
    padded[2 - 2 * core, 1 : planes + 1] = inner[...]


def conv_kernel(backward, place, pair, inner, weight, *refs):
    *outs, padded, flat = refs
    slabs = len(outs)
    rows, lanes = outs[0].shape
    height = inner.shape[1]
    planes = rows // height
    fill_padded(padded, pair, inner, place[0])
    for cell in range(9):
        for r in range(3):
            if backward:
                flat[r * lanes : (r + 1) * lanes, cell * lanes : (cell + 1) * lanes] = weight[3 * cell + r]
            else:
                flat[cell * lanes : (cell + 1) * lanes, r * lanes : (r + 1) * lanes] = weight[3 * cell + r]
    for step, out in enumerate(outs):
        slab = lax.rem(place[1] + step, slabs)
        pieces = []
        for p in range(3):
            for q in range(3):
                column, plane = (2 - p, 2 - q) if backward else (p, q)
                start = slab * planes + plane
                pieces.append(padded[column, pl.ds(start, planes)].reshape(rows, lanes))
        lhs = jnp.concatenate(pieces, axis=1)
        dims = (((1,), (1 if backward else 0,)), ((), ()))
        taps = lax.dot_general(lhs, flat[...], dims, preferred_element_type=F32)
        low, high = (2, 0) if backward else (0, 2)
        total = taps[:, lanes : 2 * lanes]
        total += shifted(taps[:, low * lanes : (low + 1) * lanes], height, -1)
        total += shifted(taps[:, high * lanes : (high + 1) * lanes], height, 1)
        out[...] = total


def convolve(backward, core, me, pair, inner, weight, slabs):
    planes, height, lanes = inner.shape
    rows = planes * height
    flat = (3 * lanes, 9 * lanes) if backward else (9 * lanes, 3 * lanes)
    return pl.pallas_call(
        functools.partial(conv_kernel, backward),
        out_shape=[jax.ShapeDtypeStruct((rows // slabs, lanes), F32)] * slabs,
        in_specs=[SMEM, VMEM, VMEM, VMEM],
        out_specs=[VMEM] * slabs,
        scratch_shapes=[
            pltpu.VMEM((3, planes + 2, height, lanes), BF16),
            pltpu.VMEM(flat, BF16),
        ],
        compiler_params=pltpu.CompilerParams(vmem_limit_bytes=14 << 20),
        cost_estimate=pl.CostEstimate(
            flops=2 * 27 * rows * lanes * lanes, bytes_accessed=3 << 20, transcendentals=0
        ),
        name="input_grad" if backward else "forward",
    )(jnp.stack([core, me]), pair, inner, weight)


def filter_kernel(core, data, pair, inner, keep, send, padded, turned, taps):
    planes, height, lanes = inner.shape
    rows = planes * height
    fill_padded(padded, pair, inner, core[0])
    flat = data[:, 0].reshape(rows, lanes).astype(F32)
    turned[0:lanes] = shifted(flat, height, -1).T.astype(BF16)
    turned[lanes : 2 * lanes] = flat.T.astype(BF16)
    turned[2 * lanes : 3 * lanes] = shifted(flat, height, 1).T.astype(BF16)
    for p in range(3):
        pieces = [padded[2 - p, 2 - q : 2 - q + planes].reshape(rows, lanes) for q in range(3)]
        rhs = jnp.concatenate(pieces, axis=1)
        result = jnp.dot(turned[...], rhs, preferred_element_type=F32)
        for q in range(3):
            for r in range(3):
                tap = 9 * p + 3 * q + r
                taps[tap * lanes : (tap + 1) * lanes] = result[
                    r * lanes : (r + 1) * lanes, q * lanes : (q + 1) * lanes
                ]
    taps[27 * lanes :] = jnp.zeros((lanes, lanes), F32)
    half = keep.shape[0]

    @pl.when(core[0] == 0)
    def _():
        keep[...] = taps[0:half]
        send[...] = taps[half : 2 * half]

    @pl.when(core[0] == 1)
    def _():
        keep[...] = taps[half : 2 * half]
        send[...] = taps[0:half]


def filter_partial(core, data, pair, inner):
    planes, height, lanes = inner.shape
    rows = planes * height
    half = jax.ShapeDtypeStruct((14 * lanes, lanes), F32)
    return pl.pallas_call(
        filter_kernel,
        out_shape=(half, half),
        in_specs=[SMEM, VMEM, VMEM, VMEM],
        out_specs=(VMEM, VMEM),
        scratch_shapes=[
            pltpu.VMEM((3, planes + 2, height, lanes), BF16),
            pltpu.VMEM((3 * lanes, rows), BF16),
            pltpu.VMEM((28 * lanes, lanes), F32),
        ],
        compiler_params=pltpu.CompilerParams(vmem_limit_bytes=14 << 20),
        cost_estimate=pl.CostEstimate(
            flops=2 * 27 * rows * lanes * lanes, bytes_accessed=3 << 20, transcendentals=0
        ),
        name="filter_grad",
    )(core.reshape(1), data, pair, inner)


def exchange(block, axis):
    return lax.all_to_all(block, axis, split_axis=0, concat_axis=0, tiled=True)


def gather(block, axis):
    count = lax.axis_size(axis)
    return exchange(jnp.broadcast_to(block[None], (count, *block.shape)), axis)


def reduced(terms, axis):
    count = len(terms)
    total = terms[0]
    for step in range(1, count):
        total += lax.ppermute(terms[step], axis, [(i, (i + step) % count) for i in range(count)])
    return total


def after(value, *others):
    return lax.optimization_barrier((value, *others))[0]


def shards(sizes, activations, weight, output_grad):
    _, zhis, rings, cores, spaces = sizes
    planes, height, lanes = activations.shape[1:]
    core = lax.axis_index("core")
    swap = [(0, 1), (1, 0)]

    outer = lax.ppermute(output_grad, AXES, outer_neighbour(sizes))
    grad = jnp.concatenate([output_grad, outer], axis=0)
    grad, later = lax.optimization_barrier((grad, activations))
    grad = lax.ppermute(grad, AXES, transposed(sizes))
    outer = lax.ppermute(later, AXES, outer_neighbour(sizes))
    data = gather(jnp.concatenate([activations, outer], axis=0), "space")
    grad = lax.all_gather(after(grad, outer), "chan", axis=1, tiled=True)
    grad_inner = lax.ppermute(grad[0], "core", swap)

    keep, send = filter_partial(core, data, grad, grad_inner)
    moved = lax.ppermute(send, "core", swap)
    own = after(data[:, 0].reshape(grad_inner.shape), send)
    data_inner = lax.ppermute(own, "core", swap)
    half, data_inner = lax.optimization_barrier((keep + moved, data_inner))

    moved = exchange(half.reshape(rings, -1, lanes), "ring")
    me = lax.axis_index("space")
    back = convolve(True, core, me, after(grad, half), grad_inner, weight, spaces)
    input_grad = reduced(back, "space").astype(BF16).reshape(activations.shape)
    quarter, input_grad = lax.optimization_barrier((moved.sum(0), input_grad))

    moved = exchange(quarter.reshape(zhis, -1, lanes), "zhi")
    me = lax.axis_index("chan")
    forward = convolve(False, core, me, after(data, quarter), data_inner, weight, spaces)
    forward = reduced(forward, "chan").astype(BF16)
    cell_count = sizes[1] * rings * cores * grad.shape[1] * grad.shape[2]
    part = moved.sum(0) / math.sqrt(cell_count)
    part, forward = lax.optimization_barrier((part, forward))

    quarter = gather(part, "zhi").reshape(-1, lanes)
    output = lax.ppermute(forward, AXES, transposed(sizes)).reshape(activations.shape)
    quarter, output = lax.optimization_barrier((quarter, output))

    half = gather(quarter, "ring").reshape(-1, lanes)

    other = lax.ppermute(half, "core", swap)
    first = core == 0
    low = jnp.where(first, half, other)
    high = jnp.where(first, other, half)
    taps = weight.shape[0]
    filter_grad = jnp.concatenate([low, high[: taps * lanes - low.shape[0]]], axis=0)
    filter_grad = filter_grad.reshape(weight.shape)
    return output, input_grad, filter_grad


def solution(mesh):
    chans, filts, spaces = (mesh.shape[name] for name in ("chan", "filt", "space"))
    sizes = (chans, filts // 8, 4, 2, spaces)
    fine = Mesh(mesh.devices.reshape(sizes), AXES)
    cells = P(("zhi", "ring", "core"), "space", None, "chan")
    filters = P(None, "chan", "space")
    return jax.shard_map(
        functools.partial(shards, sizes),
        mesh=fine,
        in_specs=(cells, filters, cells),
        out_specs=(cells, cells, filters),
        check_vma=False,
    )
```

```python
import functools
import math

import jax
import jax.numpy as jnp
import numpy as np
from jax import lax
from jax.experimental import pallas as pl
from jax.experimental.pallas import tpu as pltpu
from jax.sharding import Mesh, PartitionSpec as P

AXES = ("chan", "zhi", "ring", "core", "space")
F32 = jnp.float32
BF16 = jnp.bfloat16
VMEM = pl.BlockSpec(memory_space=pltpu.VMEM)
SMEM = pl.BlockSpec(memory_space=pltpu.SMEM)


def permutation(sizes, move):
    pairs = []
    for source in range(math.prod(sizes)):
        target = move(*(int(v) for v in np.unravel_index(source, sizes)))
        if target is not None:
            pairs.append((source, int(np.ravel_multi_index(target, sizes))))
    return pairs


def outer_neighbour(sizes):
    _, zhis, rings, cores, _ = sizes

    def move(chan, zhi, ring, core, space):
        column = (zhi * rings + ring) * cores + core
        column += 1 if column % 2 else -1
        if not 0 <= column < zhis * rings * cores:
            return None
        return (chan, column // (rings * cores), column // cores % rings, column % cores, space)

    return permutation(sizes, move)


def transposed(sizes):
    return permutation(sizes, lambda chan, zhi, ring, core, space: (space, zhi, ring, core, chan))


def height_mask(rows, height, at):
    return lax.broadcasted_iota(jnp.int32, (rows, 128), 0) % height == at


def shifted(value, height, step):
    rows = value.shape[0]
    edge = 0 if step < 0 else height - 1
    rolled = pltpu.roll(value, (-step) % rows, 0)
    return jnp.where(height_mask(rows, height, edge), 0.0, rolled)


def fill_padded(padded, pair, inner, core):
    planes, height, lanes = padded.shape[1:]
    planes -= 2
    zero = jnp.zeros((3, 1, height, lanes), BF16)
    padded[:, 0:1] = zero
    padded[:, planes + 1 : planes + 2] = zero
    for column, source in ((1, 0), (2 * core, 1)):
        if len(pair.shape) == 4:
            padded[column, 1 : planes + 1] = pair[source]
        else:
            slabs, _, depth = pair.shape[:3]
            for slab in range(slabs):
                padded[column, 1 + slab * depth : 1 + (slab + 1) * depth] = pair[slab, source]
    padded[2 - 2 * core, 1 : planes + 1] = inner[...]


def conv_kernel(backward, core, pair, inner, weight, out, padded, flat):
    slabs, rows, lanes = out.shape
    height = inner.shape[1]
    planes = rows // height
    fill_padded(padded, pair, inner, core[0])
    for cell in range(9):
        for r in range(3):
            if backward:
                flat[r * lanes : (r + 1) * lanes, cell * lanes : (cell + 1) * lanes] = weight[3 * cell + r]
            else:
                flat[cell * lanes : (cell + 1) * lanes, r * lanes : (r + 1) * lanes] = weight[3 * cell + r]
    for slab in range(slabs):
        pieces = []
        for p in range(3):
            for q in range(3):
                column, plane = (2 - p, 2 - q) if backward else (p, q)
                start = slab * planes + plane
                pieces.append(padded[column, start : start + planes].reshape(rows, lanes))
        lhs = jnp.concatenate(pieces, axis=1)
        dims = (((1,), (1 if backward else 0,)), ((), ()))
        taps = lax.dot_general(lhs, flat[...], dims, preferred_element_type=F32)
        low, high = (2, 0) if backward else (0, 2)
        total = taps[:, lanes : 2 * lanes]
        total += shifted(taps[:, low * lanes : (low + 1) * lanes], height, -1)
        total += shifted(taps[:, high * lanes : (high + 1) * lanes], height, 1)
        out[slab] = total


def convolve(backward, core, pair, inner, weight, slabs):
    planes, height, lanes = inner.shape
    rows = planes * height
    flat = (3 * lanes, 9 * lanes) if backward else (9 * lanes, 3 * lanes)
    return pl.pallas_call(
        functools.partial(conv_kernel, backward),
        out_shape=jax.ShapeDtypeStruct((slabs, rows // slabs, lanes), F32),
        in_specs=[SMEM, VMEM, VMEM, VMEM],
        out_specs=VMEM,
        scratch_shapes=[
            pltpu.VMEM((3, planes + 2, height, lanes), BF16),
            pltpu.VMEM(flat, BF16),
        ],
        compiler_params=pltpu.CompilerParams(vmem_limit_bytes=14 << 20),
        cost_estimate=pl.CostEstimate(
            flops=2 * 27 * rows * lanes * lanes, bytes_accessed=3 << 20, transcendentals=0
        ),
        name="input_grad" if backward else "forward",
    )(core.reshape(1), pair, inner, weight)


def filter_kernel(core, data, pair, inner, keep, send, padded, turned, taps):
    planes, height, lanes = inner.shape
    rows = planes * height
    fill_padded(padded, pair, inner, core[0])
    flat = data[:, 0].reshape(rows, lanes).astype(F32)
    turned[0:lanes] = shifted(flat, height, -1).T.astype(BF16)
    turned[lanes : 2 * lanes] = flat.T.astype(BF16)
    turned[2 * lanes : 3 * lanes] = shifted(flat, height, 1).T.astype(BF16)
    for p in range(3):
        pieces = [padded[2 - p, 2 - q : 2 - q + planes].reshape(rows, lanes) for q in range(3)]
        rhs = jnp.concatenate(pieces, axis=1)
        result = jnp.dot(turned[...], rhs, preferred_element_type=F32)
        for q in range(3):
            for r in range(3):
                tap = 9 * p + 3 * q + r
                taps[tap * lanes : (tap + 1) * lanes] = result[
                    r * lanes : (r + 1) * lanes, q * lanes : (q + 1) * lanes
                ]
    taps[27 * lanes :] = jnp.zeros((lanes, lanes), F32)
    half = keep.shape[0]

    @pl.when(core[0] == 0)
    def _():
        keep[...] = taps[0:half]
        send[...] = taps[half : 2 * half]

    @pl.when(core[0] == 1)
    def _():
        keep[...] = taps[half : 2 * half]
        send[...] = taps[0:half]


def filter_partial(core, data, pair, inner):
    planes, height, lanes = inner.shape
    rows = planes * height
    half = jax.ShapeDtypeStruct((14 * lanes, lanes), F32)
    return pl.pallas_call(
        filter_kernel,
        out_shape=(half, half),
        in_specs=[SMEM, VMEM, VMEM, VMEM],
        out_specs=(VMEM, VMEM),
        scratch_shapes=[
            pltpu.VMEM((3, planes + 2, height, lanes), BF16),
            pltpu.VMEM((3 * lanes, rows), BF16),
            pltpu.VMEM((28 * lanes, lanes), F32),
        ],
        compiler_params=pltpu.CompilerParams(vmem_limit_bytes=14 << 20),
        cost_estimate=pl.CostEstimate(
            flops=2 * 27 * rows * lanes * lanes, bytes_accessed=3 << 20, transcendentals=0
        ),
        name="filter_grad",
    )(core.reshape(1), data, pair, inner)


def exchange(block, axis):
    return lax.all_to_all(block, axis, split_axis=0, concat_axis=0, tiled=True)


def gather(block, axis):
    count = lax.axis_size(axis)
    return exchange(jnp.broadcast_to(block[None], (count, *block.shape)), axis)


def after(value, *others):
    return lax.optimization_barrier((value, *others))[0]


def shards(sizes, activations, weight, output_grad):
    _, zhis, rings, cores, spaces = sizes
    planes, height, lanes = activations.shape[1:]
    core = lax.axis_index("core")
    swap = [(0, 1), (1, 0)]

    outer = lax.ppermute(output_grad, AXES, outer_neighbour(sizes))
    outer_data = lax.ppermute(activations, AXES, outer_neighbour(sizes))
    grad, outer_data = lax.optimization_barrier(
        (jnp.concatenate([output_grad, outer], axis=0), outer_data)
    )
    grad = lax.ppermute(grad, AXES, transposed(sizes))
    data = jnp.concatenate([activations, outer_data], axis=0)
    grad, data = lax.optimization_barrier((grad, data))
    data = gather(data, "space")
    grad = lax.all_gather(grad, "chan", axis=1, tiled=True)
    grad_inner = lax.ppermute(grad[0], "core", swap)

    keep, send = filter_partial(core, data, grad, grad_inner)
    moved = lax.ppermute(send, "core", swap)
    own = after(data[:, 0].reshape(grad_inner.shape), send)
    data_inner = lax.ppermute(own, "core", swap)
    back = convolve(True, core, after(grad, send), grad_inner, weight, spaces)
    half, data_inner, back = lax.optimization_barrier((keep + moved, data_inner, back))
    back = lax.psum_scatter(back, "space", scatter_dimension=0, tiled=True)

    moved = exchange(half.reshape(rings, -1, lanes), "ring")
    forward = convolve(False, core, after(data, half), data_inner, weight, spaces)
    quarter, forward = lax.optimization_barrier((moved.sum(0), forward))
    forward = lax.psum_scatter(forward, "chan", scatter_dimension=0, tiled=True)

    part = exchange(quarter.reshape(zhis, -1, lanes), "zhi").sum(0)
    cell_count = sizes[1] * rings * cores * grad.shape[1] * grad.shape[2]
    part, back = lax.optimization_barrier((part / math.sqrt(cell_count), back))
    quarter, forward = lax.optimization_barrier((gather(part, "zhi").reshape(-1, lanes), forward))

    half = gather(quarter, "ring").reshape(-1, lanes)
    output = lax.ppermute(forward[0].astype(BF16), AXES, transposed(sizes))
    output = output.reshape(activations.shape)
    input_grad = back[0].astype(BF16).reshape(activations.shape)
    half, output, input_grad = lax.optimization_barrier((half, output, input_grad))

    other = lax.ppermute(half, "core", swap)
    first = core == 0
    low = jnp.where(first, half, other)
    high = jnp.where(first, other, half)
    taps = weight.shape[0]
    filter_grad = jnp.concatenate([low, high[: taps * lanes - low.shape[0]]], axis=0)
    filter_grad = filter_grad.reshape(weight.shape)
    return output, input_grad, filter_grad


def solution(mesh):
    chans, filts, spaces = (mesh.shape[name] for name in ("chan", "filt", "space"))
    sizes = (chans, filts // 8, 4, 2, spaces)
    fine = Mesh(mesh.devices.reshape(sizes), AXES)
    cells = P(("zhi", "ring", "core"), "space", None, "chan")
    filters = P(None, "chan", "space")
    return jax.shard_map(
        functools.partial(shards, sizes),
        mesh=fine,
        in_specs=(cells, filters, cells),
        out_specs=(cells, cells, filters),
        check_vma=False,
    )
```

```python
import functools
import math

import jax
import jax.numpy as jnp
import numpy as np
from jax import lax
from jax.experimental import pallas as pl
from jax.experimental.pallas import tpu as pltpu
from jax.sharding import Mesh, PartitionSpec as P

AXES = ("chan", "zhi", "ring", "core", "space")
F32 = jnp.float32
BF16 = jnp.bfloat16
VMEM = pl.BlockSpec(memory_space=pltpu.VMEM)
SMEM = pl.BlockSpec(memory_space=pltpu.SMEM)


def permutation(sizes, move):
    pairs = []
    for source in range(math.prod(sizes)):
        target = move(*(int(v) for v in np.unravel_index(source, sizes)))
        if target is not None:
            pairs.append((source, int(np.ravel_multi_index(target, sizes))))
    return pairs


def outer_neighbour(sizes):
    _, zhis, rings, cores, _ = sizes

    def move(chan, zhi, ring, core, space):
        column = (zhi * rings + ring) * cores + core
        column += 1 if column % 2 else -1
        if not 0 <= column < zhis * rings * cores:
            return None
        return (chan, column // (rings * cores), column // cores % rings, column % cores, space)

    return permutation(sizes, move)


def transposed(sizes):
    return permutation(sizes, lambda chan, zhi, ring, core, space: (space, zhi, ring, core, chan))


def height_mask(rows, height, at):
    return lax.broadcasted_iota(jnp.int32, (rows, 128), 0) % height == at


def shifted(value, height, step):
    rows = value.shape[0]
    edge = 0 if step < 0 else height - 1
    rolled = pltpu.roll(value, (-step) % rows, 0)
    return jnp.where(height_mask(rows, height, edge), 0.0, rolled)


def fill_padded(padded, pair, inner, core):
    planes, height, lanes = padded.shape[1:]
    planes -= 2
    zero = jnp.zeros((3, 1, height, lanes), BF16)
    padded[:, 0:1] = zero
    padded[:, planes + 1 : planes + 2] = zero
    for column, source in ((1, 0), (2 * core, 1)):
        if len(pair.shape) == 4:
            padded[column, 1 : planes + 1] = pair[source]
        else:
            slabs, _, depth = pair.shape[:3]
            for slab in range(slabs):
                padded[column, 1 + slab * depth : 1 + (slab + 1) * depth] = pair[slab, source]
    padded[2 - 2 * core, 1 : planes + 1] = inner[...]


def conv_kernel(backward, place, pair, inner, weight, *refs):
    *outs, padded, flat = refs
    slabs = len(outs)
    rows, lanes = outs[0].shape
    height = inner.shape[1]
    planes = rows // height
    fill_padded(padded, pair, inner, place[0])
    for cell in range(9):
        for r in range(3):
            if backward:
                flat[r * lanes : (r + 1) * lanes, cell * lanes : (cell + 1) * lanes] = weight[3 * cell + r]
            else:
                flat[cell * lanes : (cell + 1) * lanes, r * lanes : (r + 1) * lanes] = weight[3 * cell + r]
    for step, out in enumerate(outs):
        slab = lax.rem(place[1] + step, slabs)
        pieces = []
        for p in range(3):
            for q in range(3):
                column, plane = (2 - p, 2 - q) if backward else (p, q)
                start = slab * planes + plane
                pieces.append(padded[column, pl.ds(start, planes)].reshape(rows, lanes))
        lhs = jnp.concatenate(pieces, axis=1)
        dims = (((1,), (1 if backward else 0,)), ((), ()))
        taps = lax.dot_general(lhs, flat[...], dims, preferred_element_type=F32)
        low, high = (2, 0) if backward else (0, 2)
        total = taps[:, lanes : 2 * lanes]
        total += shifted(taps[:, low * lanes : (low + 1) * lanes], height, -1)
        total += shifted(taps[:, high * lanes : (high + 1) * lanes], height, 1)
        out[...] = total


def convolve(backward, core, me, pair, inner, weight, slabs):
    planes, height, lanes = inner.shape
    rows = planes * height
    flat = (3 * lanes, 9 * lanes) if backward else (9 * lanes, 3 * lanes)
    return pl.pallas_call(
        functools.partial(conv_kernel, backward),
        out_shape=[jax.ShapeDtypeStruct((rows // slabs, lanes), F32)] * slabs,
        in_specs=[SMEM, VMEM, VMEM, VMEM],
        out_specs=[VMEM] * slabs,
        scratch_shapes=[
            pltpu.VMEM((3, planes + 2, height, lanes), BF16),
            pltpu.VMEM(flat, BF16),
        ],
        compiler_params=pltpu.CompilerParams(vmem_limit_bytes=14 << 20),
        cost_estimate=pl.CostEstimate(
            flops=2 * 27 * rows * lanes * lanes, bytes_accessed=3 << 20, transcendentals=0
        ),
        name="input_grad" if backward else "forward",
    )(jnp.stack([core, me]), pair, inner, weight)


def filter_kernel(core, data, pair, inner, keep, send, padded, turned, taps):
    planes, height, lanes = inner.shape
    rows = planes * height
    fill_padded(padded, pair, inner, core[0])
    flat = data[:, 0].reshape(rows, lanes).astype(F32)
    turned[0:lanes] = shifted(flat, height, -1).T.astype(BF16)
    turned[lanes : 2 * lanes] = flat.T.astype(BF16)
    turned[2 * lanes : 3 * lanes] = shifted(flat, height, 1).T.astype(BF16)
    for p in range(3):
        pieces = [padded[2 - p, 2 - q : 2 - q + planes].reshape(rows, lanes) for q in range(3)]
        rhs = jnp.concatenate(pieces, axis=1)
        result = jnp.dot(turned[...], rhs, preferred_element_type=F32)
        for q in range(3):
            for r in range(3):
                tap = 9 * p + 3 * q + r
                taps[tap * lanes : (tap + 1) * lanes] = result[
                    r * lanes : (r + 1) * lanes, q * lanes : (q + 1) * lanes
                ]
    taps[27 * lanes :] = jnp.zeros((lanes, lanes), F32)
    half = keep.shape[0]

    @pl.when(core[0] == 0)
    def _():
        keep[...] = taps[0:half]
        send[...] = taps[half : 2 * half]

    @pl.when(core[0] == 1)
    def _():
        keep[...] = taps[half : 2 * half]
        send[...] = taps[0:half]


def filter_partial(core, data, pair, inner):
    planes, height, lanes = inner.shape
    rows = planes * height
    half = jax.ShapeDtypeStruct((14 * lanes, lanes), F32)
    return pl.pallas_call(
        filter_kernel,
        out_shape=(half, half),
        in_specs=[SMEM, VMEM, VMEM, VMEM],
        out_specs=(VMEM, VMEM),
        scratch_shapes=[
            pltpu.VMEM((3, planes + 2, height, lanes), BF16),
            pltpu.VMEM((3 * lanes, rows), BF16),
            pltpu.VMEM((28 * lanes, lanes), F32),
        ],
        compiler_params=pltpu.CompilerParams(vmem_limit_bytes=14 << 20),
        cost_estimate=pl.CostEstimate(
            flops=2 * 27 * rows * lanes * lanes, bytes_accessed=3 << 20, transcendentals=0
        ),
        name="filter_grad",
    )(core.reshape(1), data, pair, inner)


def exchange(block, axis):
    return lax.all_to_all(block, axis, split_axis=0, concat_axis=0, tiled=True)


def gather(block, axis):
    count = lax.axis_size(axis)
    return exchange(jnp.broadcast_to(block[None], (count, *block.shape)), axis)


def rotate(term, axis, step):
    count = lax.axis_size(axis)
    return lax.ppermute(term, axis, [(i, (i + step) % count) for i in range(count)])


def after(value, *others):
    return lax.optimization_barrier((value, *others))[0]


def shards(sizes, activations, weight, output_grad):
    _, zhis, rings, cores, spaces = sizes
    planes, height, lanes = activations.shape[1:]
    core = lax.axis_index("core")
    swap = [(0, 1), (1, 0)]

    outer = lax.ppermute(output_grad, AXES, outer_neighbour(sizes))
    outer_data = lax.ppermute(activations, AXES, outer_neighbour(sizes))
    grad, outer_data = lax.optimization_barrier(
        (jnp.concatenate([output_grad, outer], axis=0), outer_data)
    )
    grad = lax.ppermute(grad, AXES, transposed(sizes))
    data = jnp.concatenate([activations, outer_data], axis=0)
    grad, data = lax.optimization_barrier((grad, data))
    data = gather(data, "space")
    grad = lax.all_gather(grad, "chan", axis=1, tiled=True)
    grad_inner = lax.ppermute(grad[0], "core", swap)

    keep, send = filter_partial(core, data, grad, grad_inner)
    half = keep + lax.ppermute(send, "core", swap)

    moved = exchange(half.reshape(rings, -1, lanes), "ring")
    me = lax.axis_index("space")
    back = convolve(True, core, me, after(grad, half), grad_inner, weight, spaces)
    back = [back[0], rotate(back[1], "space", 1), rotate(back[2], "space", 2), back[3]]
    quarter, *back = lax.optimization_barrier((moved.sum(0), *back))

    moved = exchange(quarter.reshape(zhis, -1, lanes), "zhi")
    own = after(data[:, 0].reshape(grad_inner.shape), quarter)
    data_inner = lax.ppermute(own, "core", swap)
    me = lax.axis_index("chan")
    forward = convolve(False, core, me, after(data, quarter), data_inner, weight, spaces)
    forward = [forward[0], rotate(forward[1], "chan", 1), *forward[2:]]
    back[3] = rotate(back[3], "space", 3)
    cell_count = sizes[1] * rings * cores * grad.shape[1] * grad.shape[2]
    part = moved.sum(0) / math.sqrt(cell_count)
    part, back, forward = lax.optimization_barrier((part, back, forward))

    quarter = gather(part, "zhi").reshape(-1, lanes)
    forward = [*forward[:2], rotate(forward[2], "chan", 2), rotate(forward[3], "chan", 3)]
    input_grad = sum(back).astype(BF16).reshape(activations.shape)
    quarter, forward, input_grad = lax.optimization_barrier((quarter, forward, input_grad))

    half = gather(quarter, "ring").reshape(-1, lanes)
    output = lax.ppermute(sum(forward).astype(BF16), AXES, transposed(sizes))
    output = output.reshape(activations.shape)
    half, output = lax.optimization_barrier((half, output))

    other = lax.ppermute(half, "core", swap)
    first = core == 0
    low = jnp.where(first, half, other)
    high = jnp.where(first, other, half)
    taps = weight.shape[0]
    filter_grad = jnp.concatenate([low, high[: taps * lanes - low.shape[0]]], axis=0)
    filter_grad = filter_grad.reshape(weight.shape)
    return output, input_grad, filter_grad


def solution(mesh):
    chans, filts, spaces = (mesh.shape[name] for name in ("chan", "filt", "space"))
    sizes = (chans, filts // 8, 4, 2, spaces)
    fine = Mesh(mesh.devices.reshape(sizes), AXES)
    cells = P(("zhi", "ring", "core"), "space", None, "chan")
    filters = P(None, "chan", "space")
    return jax.shard_map(
        functools.partial(shards, sizes),
        mesh=fine,
        in_specs=(cells, filters, cells),
        out_specs=(cells, cells, filters),
        check_vma=False,
    )
```

```python
import functools
import math

import jax
import jax.numpy as jnp
import numpy as np
from jax import lax
from jax.experimental import pallas as pl
from jax.experimental.pallas import tpu as pltpu
from jax.sharding import Mesh, PartitionSpec as P

AXES = ("chan", "zhi", "ring", "core", "space")
F32 = jnp.float32
BF16 = jnp.bfloat16
VMEM = pl.BlockSpec(memory_space=pltpu.VMEM)
SMEM = pl.BlockSpec(memory_space=pltpu.SMEM)


def permutation(sizes, move):
    pairs = []
    for source in range(math.prod(sizes)):
        target = move(*(int(v) for v in np.unravel_index(source, sizes)))
        if target is not None:
            pairs.append((source, int(np.ravel_multi_index(target, sizes))))
    return pairs


def neighbour(sizes, outer, turn):
    _, zhis, rings, cores, _ = sizes

    def move(chan, zhi, ring, core, space):
        column = (zhi * rings + ring) * cores + core
        if outer:
            column += 1 if column % 2 else -1
        if not 0 <= column < zhis * rings * cores:
            return None
        if turn:
            chan, space = space, chan
        return (chan, column // (rings * cores), column // cores % rings, column % cores, space)

    return permutation(sizes, move)


def height_mask(rows, height, at):
    return lax.broadcasted_iota(jnp.int32, (rows, 128), 0) % height == at


def shifted(value, height, step):
    rows = value.shape[0]
    edge = 0 if step < 0 else height - 1
    rolled = pltpu.roll(value, (-step) % rows, 0)
    return jnp.where(height_mask(rows, height, edge), 0.0, rolled)


def fill_padded(padded, pair, inner, core):
    planes, height, lanes = padded.shape[1:]
    planes -= 2
    zero = jnp.zeros((3, 1, height, lanes), BF16)
    padded[:, 0:1] = zero
    padded[:, planes + 1 : planes + 2] = zero
    for column, source in ((1, 0), (2 * core, 1)):
        if len(pair.shape) == 4:
            padded[column, 1 : planes + 1] = pair[source]
        else:
            slabs, _, depth = pair.shape[:3]
            for slab in range(slabs):
                padded[column, 1 + slab * depth : 1 + (slab + 1) * depth] = pair[slab, source]
    padded[2 - 2 * core, 1 : planes + 1] = inner[...]


def conv_kernel(backward, place, pair, inner, weight, *refs):
    *outs, padded, flat = refs
    slabs = len(outs)
    rows, lanes = outs[0].shape
    height = inner.shape[1]
    planes = rows // height
    fill_padded(padded, pair, inner, place[0])
    for cell in range(9):
        for r in range(3):
            if backward:
                flat[r * lanes : (r + 1) * lanes, cell * lanes : (cell + 1) * lanes] = weight[3 * cell + r]
            else:
                flat[cell * lanes : (cell + 1) * lanes, r * lanes : (r + 1) * lanes] = weight[3 * cell + r]
    for step, out in enumerate(outs):
        slab = lax.rem(place[1] + step, slabs)
        pieces = []
        for p in range(3):
            for q in range(3):
                column, plane = (2 - p, 2 - q) if backward else (p, q)
                start = slab * planes + plane
                pieces.append(padded[column, pl.ds(start, planes)].reshape(rows, lanes))
        lhs = jnp.concatenate(pieces, axis=1)
        dims = (((1,), (1 if backward else 0,)), ((), ()))
        taps = lax.dot_general(lhs, flat[...], dims, preferred_element_type=F32)
        low, high = (2, 0) if backward else (0, 2)
        total = taps[:, lanes : 2 * lanes]
        total += shifted(taps[:, low * lanes : (low + 1) * lanes], height, -1)
        total += shifted(taps[:, high * lanes : (high + 1) * lanes], height, 1)
        out[...] = total


def convolve(backward, core, me, pair, inner, weight, slabs):
    planes, height, lanes = inner.shape
    rows = planes * height
    flat = (3 * lanes, 9 * lanes) if backward else (9 * lanes, 3 * lanes)
    return pl.pallas_call(
        functools.partial(conv_kernel, backward),
        out_shape=[jax.ShapeDtypeStruct((rows // slabs, lanes), F32)] * slabs,
        in_specs=[SMEM, VMEM, VMEM, VMEM],
        out_specs=[VMEM] * slabs,
        scratch_shapes=[
            pltpu.VMEM((3, planes + 2, height, lanes), BF16),
            pltpu.VMEM(flat, BF16),
        ],
        compiler_params=pltpu.CompilerParams(vmem_limit_bytes=14 << 20),
        cost_estimate=pl.CostEstimate(
            flops=2 * 27 * rows * lanes * lanes, bytes_accessed=3 << 20, transcendentals=0
        ),
        name="input_grad" if backward else "forward",
    )(jnp.stack([core, me]), pair, inner, weight)


def filter_kernel(core, data, pair, inner, keep, send, own, padded, turned, taps):
    planes, height, lanes = inner.shape
    rows = planes * height
    fill_padded(padded, pair, inner, core[0])
    own[...] = data[:, 0].reshape(own.shape)
    flat = data[:, 0].reshape(rows, lanes).astype(F32)
    turned[0:lanes] = shifted(flat, height, -1).T.astype(BF16)
    turned[lanes : 2 * lanes] = flat.T.astype(BF16)
    turned[2 * lanes : 3 * lanes] = shifted(flat, height, 1).T.astype(BF16)
    for p in range(3):
        pieces = [padded[2 - p, 2 - q : 2 - q + planes].reshape(rows, lanes) for q in range(3)]
        rhs = jnp.concatenate(pieces, axis=1)
        result = jnp.dot(turned[...], rhs, preferred_element_type=F32)
        for q in range(3):
            for r in range(3):
                tap = 9 * p + 3 * q + r
                taps[tap * lanes : (tap + 1) * lanes] = result[
                    r * lanes : (r + 1) * lanes, q * lanes : (q + 1) * lanes
                ]
    taps[27 * lanes :] = jnp.zeros((lanes, lanes), F32)
    half = keep.shape[0]

    @pl.when(core[0] == 0)
    def _():
        keep[...] = taps[0:half]
        send[...] = taps[half : 2 * half]

    @pl.when(core[0] == 1)
    def _():
        keep[...] = taps[half : 2 * half]
        send[...] = taps[0:half]


def filter_partial(core, data, pair, inner):
    planes, height, lanes = inner.shape
    rows = planes * height
    half = jax.ShapeDtypeStruct((14 * lanes, lanes), F32)
    return pl.pallas_call(
        filter_kernel,
        out_shape=(half, half, jax.ShapeDtypeStruct(inner.shape, BF16)),
        in_specs=[SMEM, VMEM, VMEM, VMEM],
        out_specs=(VMEM, VMEM, VMEM),
        scratch_shapes=[
            pltpu.VMEM((3, planes + 2, height, lanes), BF16),
            pltpu.VMEM((3 * lanes, rows), BF16),
            pltpu.VMEM((28 * lanes, lanes), F32),
        ],
        compiler_params=pltpu.CompilerParams(vmem_limit_bytes=14 << 20),
        cost_estimate=pl.CostEstimate(
            flops=2 * 27 * rows * lanes * lanes, bytes_accessed=3 << 20, transcendentals=0
        ),
        name="filter_grad",
    )(core.reshape(1), data, pair, inner)


def exchange(block, axis):
    return lax.all_to_all(block, axis, split_axis=0, concat_axis=0, tiled=True)


def gather(block, axis):
    count = lax.axis_size(axis)
    return exchange(jnp.broadcast_to(block[None], (count, *block.shape)), axis)


def rotate(term, axis, step):
    count = lax.axis_size(axis)
    return lax.ppermute(term, axis, [(i, (i + step) % count) for i in range(count)])


def after(value, *others):
    return lax.optimization_barrier((value, *others))[0]


def shards(sizes, activations, weight, output_grad):
    _, zhis, rings, cores, spaces = sizes
    planes, height, lanes = activations.shape[1:]
    core = lax.axis_index("core")
    swap = [(0, 1), (1, 0)]

    outer = lax.ppermute(activations, AXES, neighbour(sizes, True, False))
    grads = [lax.ppermute(output_grad, AXES, neighbour(sizes, far, True)) for far in (False, True)]
    grad = jnp.concatenate(grads, axis=0)
    data = jnp.concatenate([activations, outer], axis=0)
    grad, data = lax.optimization_barrier((grad, data))
    data = gather(data, "space")
    grad = lax.all_gather(grad, "chan", axis=1, tiled=True)
    grad_inner = lax.ppermute(grad[0], "core", swap)

    keep, send, own = filter_partial(core, data, grad, grad_inner)
    moved = lax.ppermute(send, "core", swap)
    data_inner = lax.ppermute(after(own, send), "core", swap)
    half, data_inner = lax.optimization_barrier((keep + moved, data_inner))

    moved = exchange(half.reshape(rings, -1, lanes), "ring")
    me = lax.axis_index("space")
    back = convolve(True, core, me, after(grad, half), grad_inner, weight, spaces)
    back = [back[0], rotate(back[1], "space", 1), rotate(back[2], "space", 2), back[3]]
    quarter, *back = lax.optimization_barrier((moved.sum(0), *back))

    moved = exchange(quarter.reshape(zhis, -1, lanes), "zhi")
    me = lax.axis_index("chan")
    forward = convolve(False, core, me, after(data, quarter), data_inner, weight, spaces)
    forward = [forward[0], rotate(forward[1], "chan", 1), *forward[2:]]
    back[3] = rotate(back[3], "space", 3)
    cell_count = sizes[1] * rings * cores * grad.shape[1] * grad.shape[2]
    part = moved.sum(0) / math.sqrt(cell_count)
    part, back, forward = lax.optimization_barrier((part, back, forward))

    quarter = gather(part, "zhi").reshape(-1, lanes)
    forward = [*forward[:2], rotate(forward[2], "chan", 2), rotate(forward[3], "chan", 3)]
    input_grad = sum(back).astype(BF16).reshape(activations.shape)
    quarter, forward, _ = lax.optimization_barrier((quarter, forward, input_grad))

    half = gather(quarter, "ring").reshape(-1, lanes)
    output = lax.ppermute(
        sum(forward).astype(BF16).reshape(activations.shape), AXES, neighbour(sizes, False, True)
    )
    half = after(half, output)

    other = lax.ppermute(half, "core", swap)
    first = core == 0
    low = jnp.where(first, half, other)
    high = jnp.where(first, other, half)
    taps = weight.shape[0]
    filter_grad = jnp.concatenate([low, high[: taps * lanes - low.shape[0]]], axis=0)
    filter_grad = filter_grad.reshape(weight.shape)
    return output, input_grad, filter_grad


def solution(mesh):
    chans, filts, spaces = (mesh.shape[name] for name in ("chan", "filt", "space"))
    sizes = (chans, filts // 8, 4, 2, spaces)
    fine = Mesh(mesh.devices.reshape(sizes), AXES)
    cells = P(("zhi", "ring", "core"), "space", None, "chan")
    filters = P(None, "chan", "space")
    return jax.shard_map(
        functools.partial(shards, sizes),
        mesh=fine,
        in_specs=(cells, filters, cells),
        out_specs=(cells, cells, filters),
        check_vma=False,
    )
```

```python
import functools
import math

import jax
import jax.numpy as jnp
import numpy as np
from jax import lax
from jax.experimental import pallas as pl
from jax.experimental.pallas import tpu as pltpu
from jax.sharding import Mesh, PartitionSpec as P

AXES = ("chan", "zhi", "ring", "core", "space")
F32 = jnp.float32
BF16 = jnp.bfloat16
VMEM = pl.BlockSpec(memory_space=pltpu.VMEM)
SMEM = pl.BlockSpec(memory_space=pltpu.SMEM)


def permutation(sizes, move):
    pairs = []
    for source in range(math.prod(sizes)):
        target = move(*(int(v) for v in np.unravel_index(source, sizes)))
        if target is not None:
            pairs.append((source, int(np.ravel_multi_index(target, sizes))))
    return pairs


def neighbour(sizes, outer, turn):
    _, zhis, rings, cores, _ = sizes

    def move(chan, zhi, ring, core, space):
        column = (zhi * rings + ring) * cores + core
        if outer:
            column += 1 if column % 2 else -1
        if not 0 <= column < zhis * rings * cores:
            return None
        if turn:
            chan, space = space, chan
        return (chan, column // (rings * cores), column // cores % rings, column % cores, space)

    return permutation(sizes, move)


def height_mask(rows, height, at):
    return lax.broadcasted_iota(jnp.int32, (rows, 128), 0) % height == at


def shifted(value, height, step):
    rows = value.shape[0]
    edge = 0 if step < 0 else height - 1
    rolled = pltpu.roll(value, (-step) % rows, 0)
    return jnp.where(height_mask(rows, height, edge), 0.0, rolled)


def fill_padded(padded, pair, inner, core):
    planes, height, lanes = padded.shape[1:]
    planes -= 2
    zero = jnp.zeros((3, 1, height, lanes), BF16)
    padded[:, 0:1] = zero
    padded[:, planes + 1 : planes + 2] = zero
    for column, source in ((1, 0), (2 * core, 1)):
        if len(pair.shape) == 4:
            padded[column, 1 : planes + 1] = pair[source]
        else:
            slabs, _, depth = pair.shape[:3]
            for slab in range(slabs):
                padded[column, 1 + slab * depth : 1 + (slab + 1) * depth] = pair[slab, source]
    padded[2 - 2 * core, 1 : planes + 1] = inner[...]


def conv_kernel(backward, place, pair, inner, weight, *refs):
    *outs, padded, flat = refs
    slabs = len(outs)
    rows, lanes = outs[0].shape
    height = inner.shape[1]
    planes = rows // height
    fill_padded(padded, pair, inner, place[0])
    for cell in range(9):
        for r in range(3):
            if backward:
                flat[r * lanes : (r + 1) * lanes, cell * lanes : (cell + 1) * lanes] = weight[3 * cell + r]
            else:
                flat[cell * lanes : (cell + 1) * lanes, r * lanes : (r + 1) * lanes] = weight[3 * cell + r]
    for step, out in enumerate(outs):
        slab = lax.rem(place[1] + step, slabs)
        pieces = []
        for p in range(3):
            for q in range(3):
                column, plane = (2 - p, 2 - q) if backward else (p, q)
                start = slab * planes + plane
                pieces.append(padded[column, pl.ds(start, planes)].reshape(rows, lanes))
        lhs = jnp.concatenate(pieces, axis=1)
        dims = (((1,), (1 if backward else 0,)), ((), ()))
        taps = lax.dot_general(lhs, flat[...], dims, preferred_element_type=F32)
        low, high = (2, 0) if backward else (0, 2)
        total = taps[:, lanes : 2 * lanes]
        total += shifted(taps[:, low * lanes : (low + 1) * lanes], height, -1)
        total += shifted(taps[:, high * lanes : (high + 1) * lanes], height, 1)
        out[...] = total


def convolve(backward, core, me, pair, inner, weight, slabs):
    planes, height, lanes = inner.shape
    rows = planes * height
    flat = (3 * lanes, 9 * lanes) if backward else (9 * lanes, 3 * lanes)
    return pl.pallas_call(
        functools.partial(conv_kernel, backward),
        out_shape=[jax.ShapeDtypeStruct((rows // slabs, lanes), F32)] * slabs,
        in_specs=[SMEM, VMEM, VMEM, VMEM],
        out_specs=[VMEM] * slabs,
        scratch_shapes=[
            pltpu.VMEM((3, planes + 2, height, lanes), BF16),
            pltpu.VMEM(flat, BF16),
        ],
        compiler_params=pltpu.CompilerParams(vmem_limit_bytes=14 << 20),
        cost_estimate=pl.CostEstimate(
            flops=2 * 27 * rows * lanes * lanes, bytes_accessed=3 << 20, transcendentals=0
        ),
        name="input_grad" if backward else "forward",
    )(jnp.stack([core, me]), pair, inner, weight)


def filter_kernel(core, data, pair, inner, keep, send, own, padded, turned, taps):
    planes, height, lanes = inner.shape
    rows = planes * height
    fill_padded(padded, pair, inner, core[0])
    own[...] = data[:, 0].reshape(own.shape)
    flat = data[:, 0].reshape(rows, lanes).astype(F32)
    turned[0:lanes] = shifted(flat, height, -1).T.astype(BF16)
    turned[lanes : 2 * lanes] = flat.T.astype(BF16)
    turned[2 * lanes : 3 * lanes] = shifted(flat, height, 1).T.astype(BF16)
    for p in range(3):
        pieces = [padded[2 - p, 2 - q : 2 - q + planes].reshape(rows, lanes) for q in range(3)]
        rhs = jnp.concatenate(pieces, axis=1)
        result = jnp.dot(turned[...], rhs, preferred_element_type=F32)
        for q in range(3):
            for r in range(3):
                tap = 9 * p + 3 * q + r
                taps[tap * lanes : (tap + 1) * lanes] = result[
                    r * lanes : (r + 1) * lanes, q * lanes : (q + 1) * lanes
                ]
    taps[27 * lanes :] = jnp.zeros((lanes, lanes), F32)
    half = keep.shape[0]

    @pl.when(core[0] == 0)
    def _():
        keep[...] = taps[0:half]
        send[...] = taps[half : 2 * half]

    @pl.when(core[0] == 1)
    def _():
        keep[...] = taps[half : 2 * half]
        send[...] = taps[0:half]


def filter_partial(core, data, pair, inner):
    planes, height, lanes = inner.shape
    rows = planes * height
    half = jax.ShapeDtypeStruct((14 * lanes, lanes), F32)
    return pl.pallas_call(
        filter_kernel,
        out_shape=(half, half, jax.ShapeDtypeStruct(inner.shape, BF16)),
        in_specs=[SMEM, VMEM, VMEM, VMEM],
        out_specs=(VMEM, VMEM, VMEM),
        scratch_shapes=[
            pltpu.VMEM((3, planes + 2, height, lanes), BF16),
            pltpu.VMEM((3 * lanes, rows), BF16),
            pltpu.VMEM((28 * lanes, lanes), F32),
        ],
        compiler_params=pltpu.CompilerParams(vmem_limit_bytes=14 << 20),
        cost_estimate=pl.CostEstimate(
            flops=2 * 27 * rows * lanes * lanes, bytes_accessed=3 << 20, transcendentals=0
        ),
        name="filter_grad",
    )(core.reshape(1), data, pair, inner)


def exchange(block, axis):
    return lax.all_to_all(block, axis, split_axis=0, concat_axis=0, tiled=True)


def gather(block, axis):
    count = lax.axis_size(axis)
    return exchange(jnp.broadcast_to(block[None], (count, *block.shape)), axis)


def rotate(term, axis, step):
    count = lax.axis_size(axis)
    return lax.ppermute(term, axis, [(i, (i + step) % count) for i in range(count)])


def doubling(step):
    return [
        (2 * zhi + core, 2 * (zhi ^ 1 if core == step else 3 - zhi) + core)
        for zhi in range(4)
        for core in range(2)
    ]


def after(value, *others):
    return lax.optimization_barrier((value, *others))[0]


def shards(sizes, activations, weight, output_grad):
    _, zhis, rings, cores, spaces = sizes
    planes, height, lanes = activations.shape[1:]
    core = lax.axis_index("core")
    swap = [(0, 1), (1, 0)]

    outer = lax.ppermute(activations, AXES, neighbour(sizes, True, False))
    grads = [lax.ppermute(output_grad, AXES, neighbour(sizes, far, True)) for far in (False, True)]
    grad = jnp.concatenate(grads, axis=0)
    data = jnp.concatenate([activations, outer], axis=0)
    grad, data = lax.optimization_barrier((grad, data))
    data = gather(data, "space")
    grad = lax.all_gather(grad, "chan", axis=1, tiled=True)
    grad_inner = lax.ppermute(grad[0], "core", swap)

    keep, send, own = filter_partial(core, data, grad, grad_inner)
    moved = lax.ppermute(send, "core", swap)
    data_inner = lax.ppermute(after(own, send), "core", swap)
    half, data_inner = lax.optimization_barrier((keep + moved, data_inner))

    moved = exchange(half.reshape(rings, -1, lanes), "ring")
    me = lax.axis_index("space")
    back = convolve(True, core, me, after(grad, half), grad_inner, weight, spaces)
    back = [back[0], rotate(back[1], "space", 1), rotate(back[2], "space", 2), back[3]]
    quarter, *back = lax.optimization_barrier((moved.sum(0), *back))

    moved = lax.ppermute(quarter, ("zhi", "core"), doubling(0))
    me = lax.axis_index("chan")
    forward = convolve(False, core, me, after(data, quarter), data_inner, weight, spaces)
    forward = [forward[0], rotate(forward[1], "chan", 1), *forward[2:]]
    back[3] = rotate(back[3], "space", 3)
    cell_count = sizes[1] * rings * cores * grad.shape[1] * grad.shape[2]
    pair = quarter + moved
    pair, back, forward = lax.optimization_barrier((pair, back, forward))

    quarter = (pair + lax.ppermute(pair, ("zhi", "core"), doubling(1))) / math.sqrt(cell_count)
    forward = [*forward[:2], rotate(forward[2], "chan", 2), rotate(forward[3], "chan", 3)]
    input_grad = sum(back).astype(BF16).reshape(activations.shape)
    quarter, forward, _ = lax.optimization_barrier((quarter, forward, input_grad))

    half = gather(quarter, "ring").reshape(-1, lanes)
    output = lax.ppermute(
        sum(forward).astype(BF16).reshape(activations.shape), AXES, neighbour(sizes, False, True)
    )
    half = after(half, output)

    other = lax.ppermute(half, "core", swap)
    first = core == 0
    low = jnp.where(first, half, other)
    high = jnp.where(first, other, half)
    taps = weight.shape[0]
    filter_grad = jnp.concatenate([low, high[: taps * lanes - low.shape[0]]], axis=0)
    filter_grad = filter_grad.reshape(weight.shape)
    return output, input_grad, filter_grad


def solution(mesh):
    chans, filts, spaces = (mesh.shape[name] for name in ("chan", "filt", "space"))
    sizes = (chans, filts // 8, 4, 2, spaces)
    fine = Mesh(mesh.devices.reshape(sizes), AXES)
    cells = P(("zhi", "ring", "core"), "space", None, "chan")
    filters = P(None, "chan", "space")
    return jax.shard_map(
        functools.partial(shards, sizes),
        mesh=fine,
        in_specs=(cells, filters, cells),
        out_specs=(cells, cells, filters),
        check_vma=False,
    )
```

```python
import functools
import math

import jax
import jax.numpy as jnp
import numpy as np
from jax import lax
from jax.experimental import pallas as pl
from jax.experimental.pallas import tpu as pltpu
from jax.sharding import Mesh, PartitionSpec as P

AXES = ("chan", "zhi", "ring", "core", "space")
F32 = jnp.float32
BF16 = jnp.bfloat16
VMEM = pl.BlockSpec(memory_space=pltpu.VMEM)
SMEM = pl.BlockSpec(memory_space=pltpu.SMEM)


def permutation(sizes, move):
    pairs = []
    for source in range(math.prod(sizes)):
        target = move(*(int(v) for v in np.unravel_index(source, sizes)))
        if target is not None:
            pairs.append((source, int(np.ravel_multi_index(target, sizes))))
    return pairs


def neighbour(sizes, outer, turn):
    _, zhis, rings, cores, _ = sizes

    def move(chan, zhi, ring, core, space):
        column = (zhi * rings + ring) * cores + core
        if outer:
            column += 1 if column % 2 else -1
        if not 0 <= column < zhis * rings * cores:
            return None
        if turn:
            chan, space = space, chan
        return (chan, column // (rings * cores), column // cores % rings, column % cores, space)

    return permutation(sizes, move)


def height_mask(rows, height, at):
    return lax.broadcasted_iota(jnp.int32, (rows, 128), 0) % height == at


def shifted(value, height, step):
    rows = value.shape[0]
    edge = 0 if step < 0 else height - 1
    rolled = pltpu.roll(value, (-step) % rows, 0)
    return jnp.where(height_mask(rows, height, edge), 0.0, rolled)


def fill_padded(padded, pair, inner, core):
    planes, height, lanes = padded.shape[1:]
    planes -= 2
    zero = jnp.zeros((3, 1, height, lanes), BF16)
    padded[:, 0:1] = zero
    padded[:, planes + 1 : planes + 2] = zero
    for column, source in ((1, 0), (2 * core, 1)):
        if len(pair.shape) == 4:
            padded[column, 1 : planes + 1] = pair[source]
        else:
            slabs, _, depth = pair.shape[:3]
            for slab in range(slabs):
                padded[column, 1 + slab * depth : 1 + (slab + 1) * depth] = pair[slab, source]
    padded[2 - 2 * core, 1 : planes + 1] = inner[...]


def conv_kernel(backward, place, pair, inner, weight, *refs):
    *outs, padded, flat = refs
    slabs = len(outs)
    rows, lanes = outs[0].shape
    height = inner.shape[1]
    planes = rows // height
    fill_padded(padded, pair, inner, place[0])
    for cell in range(9):
        for r in range(3):
            if backward:
                flat[r * lanes : (r + 1) * lanes, cell * lanes : (cell + 1) * lanes] = weight[3 * cell + r]
            else:
                flat[cell * lanes : (cell + 1) * lanes, r * lanes : (r + 1) * lanes] = weight[3 * cell + r]
    for step, out in enumerate(outs):
        slab = lax.rem(place[1] + step, slabs)
        pieces = []
        for p in range(3):
            for q in range(3):
                column, plane = (2 - p, 2 - q) if backward else (p, q)
                start = slab * planes + plane
                pieces.append(padded[column, pl.ds(start, planes)].reshape(rows, lanes))
        lhs = jnp.concatenate(pieces, axis=1)
        dims = (((1,), (1 if backward else 0,)), ((), ()))
        taps = lax.dot_general(lhs, flat[...], dims, preferred_element_type=F32)
        low, high = (2, 0) if backward else (0, 2)
        total = taps[:, lanes : 2 * lanes]
        total += shifted(taps[:, low * lanes : (low + 1) * lanes], height, -1)
        total += shifted(taps[:, high * lanes : (high + 1) * lanes], height, 1)
        out[...] = total


def convolve(backward, core, me, pair, inner, weight, slabs):
    planes, height, lanes = inner.shape
    rows = planes * height
    flat = (3 * lanes, 9 * lanes) if backward else (9 * lanes, 3 * lanes)
    return pl.pallas_call(
        functools.partial(conv_kernel, backward),
        out_shape=[jax.ShapeDtypeStruct((rows // slabs, lanes), F32)] * slabs,
        in_specs=[SMEM, VMEM, VMEM, VMEM],
        out_specs=[VMEM] * slabs,
        scratch_shapes=[
            pltpu.VMEM((3, planes + 2, height, lanes), BF16),
            pltpu.VMEM(flat, BF16),
        ],
        compiler_params=pltpu.CompilerParams(vmem_limit_bytes=14 << 20),
        cost_estimate=pl.CostEstimate(
            flops=2 * 27 * rows * lanes * lanes, bytes_accessed=3 << 20, transcendentals=0
        ),
        name="input_grad" if backward else "forward",
    )(jnp.stack([core, me]), pair, inner, weight)


def filter_kernel(core, data, pair, inner, keep, send, own, padded, turned, taps):
    planes, height, lanes = inner.shape
    rows = planes * height
    fill_padded(padded, pair, inner, core[0])
    own[...] = data[:, 0].reshape(own.shape)
    flat = data[:, 0].reshape(rows, lanes).astype(F32)
    turned[0:lanes] = shifted(flat, height, -1).T.astype(BF16)
    turned[lanes : 2 * lanes] = flat.T.astype(BF16)
    turned[2 * lanes : 3 * lanes] = shifted(flat, height, 1).T.astype(BF16)
    for p in range(3):
        pieces = [padded[2 - p, 2 - q : 2 - q + planes].reshape(rows, lanes) for q in range(3)]
        rhs = jnp.concatenate(pieces, axis=1)
        result = jnp.dot(turned[...], rhs, preferred_element_type=F32)
        for q in range(3):
            for r in range(3):
                tap = 9 * p + 3 * q + r
                taps[tap * lanes : (tap + 1) * lanes] = result[
                    r * lanes : (r + 1) * lanes, q * lanes : (q + 1) * lanes
                ]
    taps[27 * lanes :] = jnp.zeros((lanes, lanes), F32)
    half = keep.shape[0]

    @pl.when(core[0] == 0)
    def _():
        keep[...] = taps[0:half]
        send[...] = taps[half : 2 * half]

    @pl.when(core[0] == 1)
    def _():
        keep[...] = taps[half : 2 * half]
        send[...] = taps[0:half]


def filter_partial(core, data, pair, inner):
    planes, height, lanes = inner.shape
    rows = planes * height
    half = jax.ShapeDtypeStruct((14 * lanes, lanes), F32)
    return pl.pallas_call(
        filter_kernel,
        out_shape=(half, half, jax.ShapeDtypeStruct(inner.shape, BF16)),
        in_specs=[SMEM, VMEM, VMEM, VMEM],
        out_specs=(VMEM, VMEM, VMEM),
        scratch_shapes=[
            pltpu.VMEM((3, planes + 2, height, lanes), BF16),
            pltpu.VMEM((3 * lanes, rows), BF16),
            pltpu.VMEM((28 * lanes, lanes), F32),
        ],
        compiler_params=pltpu.CompilerParams(vmem_limit_bytes=14 << 20),
        cost_estimate=pl.CostEstimate(
            flops=2 * 27 * rows * lanes * lanes, bytes_accessed=3 << 20, transcendentals=0
        ),
        name="filter_grad",
    )(core.reshape(1), data, pair, inner)


def small_call(kernel, shape, *operands):
    return pl.pallas_call(
        kernel,
        out_shape=jax.ShapeDtypeStruct(shape, F32),
        in_specs=[VMEM] * len(operands),
        out_specs=VMEM,
        compiler_params=pltpu.CompilerParams(vmem_limit_bytes=8 << 20),
        cost_estimate=pl.CostEstimate(
            flops=operands[0].size, bytes_accessed=1 << 20, transcendentals=0
        ),
    )(*operands)


def add_kernel(left, right, out):
    out[...] = left[...] + right[...]


def sum_kernel(parts, out):
    out[...] = (parts[0] + parts[1]) + (parts[2] + parts[3])


def spread_kernel(scale, left, right, out):
    total = (left[...] + right[...]) * scale
    for copy in range(out.shape[0]):
        out[copy] = total


def join_kernel(core, mine, other, out, sems):
    size, rest = mine.shape[0], out.shape[0] - mine.shape[0]

    def place(low, high):
        copies = [
            pltpu.make_async_copy(low, out.at[pl.ds(0, size)], sems.at[0]),
            pltpu.make_async_copy(high.at[pl.ds(0, rest)], out.at[pl.ds(size, rest)], sems.at[1]),
        ]
        for copy in copies:
            copy.start()
        for copy in copies:
            copy.wait()

    @pl.when(core[0] == 0)
    def _():
        place(mine, other)

    @pl.when(core[0] == 1)
    def _():
        place(other, mine)


def joined(core, mine, other, shape):
    return pl.pallas_call(
        join_kernel,
        out_shape=jax.ShapeDtypeStruct(shape, F32),
        in_specs=[SMEM, VMEM, VMEM],
        out_specs=pl.BlockSpec(memory_space=pl.ANY),
        scratch_shapes=[pltpu.SemaphoreType.DMA((2,))],
        compiler_params=pltpu.CompilerParams(vmem_limit_bytes=8 << 20),
        cost_estimate=pl.CostEstimate(flops=0, bytes_accessed=4 << 20, transcendentals=0),
        name="join",
    )(core.reshape(1), mine, other)


def exchange(block, axis):
    return lax.all_to_all(block, axis, split_axis=0, concat_axis=0, tiled=True)


def gather(block, axis):
    count = lax.axis_size(axis)
    return exchange(jnp.broadcast_to(block[None], (count, *block.shape)), axis)


def rotate(term, axis, step):
    count = lax.axis_size(axis)
    return lax.ppermute(term, axis, [(i, (i + step) % count) for i in range(count)])


def doubling(step):
    return [
        (2 * zhi + core, 2 * (zhi ^ 1 if core == step else 3 - zhi) + core)
        for zhi in range(4)
        for core in range(2)
    ]


def after(value, *others):
    return lax.optimization_barrier((value, *others))[0]


def shards(sizes, activations, weight, output_grad):
    _, zhis, rings, cores, spaces = sizes
    planes, height, lanes = activations.shape[1:]
    core = lax.axis_index("core")
    swap = [(0, 1), (1, 0)]

    outer = lax.ppermute(activations, AXES, neighbour(sizes, True, False))
    grads = [lax.ppermute(output_grad, AXES, neighbour(sizes, far, True)) for far in (False, True)]
    grad = jnp.concatenate(grads, axis=0)
    data = jnp.concatenate([activations, outer], axis=0)
    grad, data = lax.optimization_barrier((grad, data))
    data = gather(data, "space")
    grad = lax.all_gather(grad, "chan", axis=1, tiled=True)
    grad_inner = lax.ppermute(grad[0], "core", swap)

    keep, send, own = filter_partial(core, data, grad, grad_inner)
    moved = lax.ppermute(send, "core", swap)
    data_inner = lax.ppermute(after(own, send), "core", swap)
    half = small_call(add_kernel, keep.shape, keep, moved)
    half, data_inner = lax.optimization_barrier((half, data_inner))

    moved = exchange(half.reshape(rings, -1, lanes), "ring")
    me = lax.axis_index("space")
    back = convolve(True, core, me, after(grad, half), grad_inner, weight, spaces)
    back = [back[0], rotate(back[1], "space", 1), rotate(back[2], "space", 2), back[3]]
    quarter, *back = lax.optimization_barrier(
        (small_call(sum_kernel, moved.shape[1:], moved), *back)
    )

    moved = lax.ppermute(quarter, ("zhi", "core"), doubling(0))
    me = lax.axis_index("chan")
    forward = convolve(False, core, me, after(data, quarter), data_inner, weight, spaces)
    forward = [forward[0], rotate(forward[1], "chan", 1), *forward[2:]]
    back[3] = rotate(back[3], "space", 3)
    cell_count = sizes[1] * rings * cores * grad.shape[1] * grad.shape[2]
    pair = quarter + moved
    pair, back, forward = lax.optimization_barrier((pair, back, forward))

    moved = lax.ppermute(pair, ("zhi", "core"), doubling(1))
    spread = functools.partial(spread_kernel, 1 / math.sqrt(cell_count))
    quarter = small_call(spread, (rings, *pair.shape), pair, moved)
    forward = [*forward[:2], rotate(forward[2], "chan", 2), rotate(forward[3], "chan", 3)]
    input_grad = sum(back).astype(BF16).reshape(activations.shape)
    quarter, forward, _ = lax.optimization_barrier((quarter, forward, input_grad))

    half = exchange(quarter, "ring").reshape(-1, lanes)
    output = lax.ppermute(
        sum(forward).astype(BF16).reshape(activations.shape), AXES, neighbour(sizes, False, True)
    )
    half = after(half, output)

    other = lax.ppermute(half, "core", swap)
    blocks = (-1, *weight.shape[1:])
    filter_grad = joined(core, half.reshape(blocks), other.reshape(blocks), weight.shape)
    return output, input_grad, filter_grad


def solution(mesh):
    chans, filts, spaces = (mesh.shape[name] for name in ("chan", "filt", "space"))
    sizes = (chans, filts // 8, 4, 2, spaces)
    fine = Mesh(mesh.devices.reshape(sizes), AXES)
    cells = P(("zhi", "ring", "core"), "space", None, "chan")
    filters = P(None, "chan", "space")
    return jax.shard_map(
        functools.partial(shards, sizes),
        mesh=fine,
        in_specs=(cells, filters, cells),
        out_specs=(cells, cells, filters),
        check_vma=False,
    )
```

```python
import functools
import math

import jax
import jax.numpy as jnp
import numpy as np
from jax import lax
from jax.experimental import pallas as pl
from jax.experimental.pallas import tpu as pltpu
from jax.sharding import Mesh, PartitionSpec as P

AXES = ("chan", "zhi", "ring", "core", "space")
F32 = jnp.float32
BF16 = jnp.bfloat16
VMEM = pl.BlockSpec(memory_space=pltpu.VMEM)
SMEM = pl.BlockSpec(memory_space=pltpu.SMEM)


def permutation(sizes, move):
    pairs = []
    for source in range(math.prod(sizes)):
        target = move(*(int(v) for v in np.unravel_index(source, sizes)))
        if target is not None:
            pairs.append((source, int(np.ravel_multi_index(target, sizes))))
    return pairs


def neighbour(sizes, outer, turn):
    _, zhis, rings, cores, _ = sizes

    def move(chan, zhi, ring, core, space):
        column = (zhi * rings + ring) * cores + core
        if outer:
            column += 1 if column % 2 else -1
        if not 0 <= column < zhis * rings * cores:
            return None
        if turn:
            chan, space = space, chan
        return (chan, column // (rings * cores), column // cores % rings, column % cores, space)

    return permutation(sizes, move)


def height_mask(rows, height, at):
    return lax.broadcasted_iota(jnp.int32, (rows, 128), 0) % height == at


def shifted(value, height, step):
    rows = value.shape[0]
    edge = 0 if step < 0 else height - 1
    rolled = pltpu.roll(value, (-step) % rows, 0)
    return jnp.where(height_mask(rows, height, edge), 0.0, rolled)


def fill_padded(padded, pair, inner, core):
    planes, height, lanes = padded.shape[1:]
    planes -= 2
    zero = jnp.zeros((3, 1, height, lanes), BF16)
    padded[:, 0:1] = zero
    padded[:, planes + 1 : planes + 2] = zero
    for column, source in ((1, 0), (2 * core, 1)):
        if len(pair.shape) == 4:
            padded[column, 1 : planes + 1] = pair[source]
        else:
            slabs, _, depth = pair.shape[:3]
            for slab in range(slabs):
                padded[column, 1 + slab * depth : 1 + (slab + 1) * depth] = pair[slab, source]
    padded[2 - 2 * core, 1 : planes + 1] = inner[...]


def conv_kernel(backward, place, pair, inner, weight, *refs):
    *outs, padded, flat = refs
    slabs = len(outs)
    rows, lanes = outs[0].shape
    height = inner.shape[1]
    planes = rows // height
    fill_padded(padded, pair, inner, place[0])
    for cell in range(9):
        for r in range(3):
            if backward:
                flat[r * lanes : (r + 1) * lanes, cell * lanes : (cell + 1) * lanes] = weight[3 * cell + r]
            else:
                flat[cell * lanes : (cell + 1) * lanes, r * lanes : (r + 1) * lanes] = weight[3 * cell + r]
    for step, out in enumerate(outs):
        slab = lax.rem(place[1] + step, slabs)
        pieces = []
        for p in range(3):
            for q in range(3):
                column, plane = (2 - p, 2 - q) if backward else (p, q)
                start = slab * planes + plane
                pieces.append(padded[column, pl.ds(start, planes)].reshape(rows, lanes))
        lhs = jnp.concatenate(pieces, axis=1)
        dims = (((1,), (1 if backward else 0,)), ((), ()))
        taps = lax.dot_general(lhs, flat[...], dims, preferred_element_type=F32)
        low, high = (2, 0) if backward else (0, 2)
        total = taps[:, lanes : 2 * lanes]
        total += shifted(taps[:, low * lanes : (low + 1) * lanes], height, -1)
        total += shifted(taps[:, high * lanes : (high + 1) * lanes], height, 1)
        out[...] = total


def convolve(backward, core, me, pair, inner, weight, slabs):
    planes, height, lanes = inner.shape
    rows = planes * height
    flat = (3 * lanes, 9 * lanes) if backward else (9 * lanes, 3 * lanes)
    return pl.pallas_call(
        functools.partial(conv_kernel, backward),
        out_shape=[jax.ShapeDtypeStruct((rows // slabs, lanes), F32)] * slabs,
        in_specs=[SMEM, VMEM, VMEM, VMEM],
        out_specs=[VMEM] * slabs,
        scratch_shapes=[
            pltpu.VMEM((3, planes + 2, height, lanes), BF16),
            pltpu.VMEM(flat, BF16),
        ],
        compiler_params=pltpu.CompilerParams(vmem_limit_bytes=14 << 20),
        cost_estimate=pl.CostEstimate(
            flops=2 * 27 * rows * lanes * lanes, bytes_accessed=3 << 20, transcendentals=0
        ),
        name="input_grad" if backward else "forward",
    )(jnp.stack([core, me]), pair, inner, weight)


def filter_kernel(core, data, pair, inner, keep, send, own, padded, turned, taps):
    planes, height, lanes = inner.shape
    rows = planes * height
    fill_padded(padded, pair, inner, core[0])
    own[...] = data[:, 0].reshape(own.shape)
    flat = data[:, 0].reshape(rows, lanes).astype(F32)
    turned[0:lanes] = shifted(flat, height, -1).T.astype(BF16)
    turned[lanes : 2 * lanes] = flat.T.astype(BF16)
    turned[2 * lanes : 3 * lanes] = shifted(flat, height, 1).T.astype(BF16)
    for p in range(3):
        pieces = [padded[2 - p, 2 - q : 2 - q + planes].reshape(rows, lanes) for q in range(3)]
        rhs = jnp.concatenate(pieces, axis=1)
        result = jnp.dot(turned[...], rhs, preferred_element_type=F32)
        for q in range(3):
            for r in range(3):
                tap = 9 * p + 3 * q + r
                taps[tap * lanes : (tap + 1) * lanes] = result[
                    r * lanes : (r + 1) * lanes, q * lanes : (q + 1) * lanes
                ]
    taps[27 * lanes :] = jnp.zeros((lanes, lanes), F32)
    half = keep.shape[0]

    @pl.when(core[0] == 0)
    def _():
        keep[...] = taps[0:half]
        send[...] = taps[half : 2 * half]

    @pl.when(core[0] == 1)
    def _():
        keep[...] = taps[half : 2 * half]
        send[...] = taps[0:half]


def filter_partial(core, data, pair, inner):
    planes, height, lanes = inner.shape
    rows = planes * height
    half = jax.ShapeDtypeStruct((14 * lanes, lanes), F32)
    return pl.pallas_call(
        filter_kernel,
        out_shape=(half, half, jax.ShapeDtypeStruct(inner.shape, BF16)),
        in_specs=[SMEM, VMEM, VMEM, VMEM],
        out_specs=(VMEM, VMEM, VMEM),
        scratch_shapes=[
            pltpu.VMEM((3, planes + 2, height, lanes), BF16),
            pltpu.VMEM((3 * lanes, rows), BF16),
            pltpu.VMEM((28 * lanes, lanes), F32),
        ],
        compiler_params=pltpu.CompilerParams(vmem_limit_bytes=14 << 20),
        cost_estimate=pl.CostEstimate(
            flops=2 * 27 * rows * lanes * lanes, bytes_accessed=3 << 20, transcendentals=0
        ),
        name="filter_grad",
    )(core.reshape(1), data, pair, inner)


def small_call(kernel, shape, *operands):
    return pl.pallas_call(
        kernel,
        out_shape=jax.ShapeDtypeStruct(shape, F32),
        in_specs=[VMEM] * len(operands),
        out_specs=VMEM,
        compiler_params=pltpu.CompilerParams(vmem_limit_bytes=8 << 20),
        cost_estimate=pl.CostEstimate(
            flops=operands[0].size, bytes_accessed=1 << 20, transcendentals=0
        ),
    )(*operands)


def add_kernel(left, right, out):
    out[...] = left[...] + right[...]


def sum_kernel(parts, out):
    out[...] = (parts[0] + parts[1]) + (parts[2] + parts[3])


def spread_kernel(scale, left, right, out):
    total = (left[...] + right[...]) * scale
    for copy in range(out.shape[0]):
        out[copy] = total


def join_kernel(core, mine, other, out, sems):
    size, rest = mine.shape[0], out.shape[0] - mine.shape[0]

    def place(low, high):
        copies = [
            pltpu.make_async_copy(low, out.at[pl.ds(0, size)], sems.at[0]),
            pltpu.make_async_copy(high.at[pl.ds(0, rest)], out.at[pl.ds(size, rest)], sems.at[1]),
        ]
        for copy in copies:
            copy.start()
        for copy in copies:
            copy.wait()

    @pl.when(core[0] == 0)
    def _():
        place(mine, other)

    @pl.when(core[0] == 1)
    def _():
        place(other, mine)


def copy_kernel(block, out):
    out[...] = block[...]


def published(block):
    return pl.pallas_call(
        copy_kernel,
        out_shape=jax.ShapeDtypeStruct(block.shape, block.dtype),
        in_specs=[VMEM],
        out_specs=VMEM,
        compiler_params=pltpu.CompilerParams(vmem_limit_bytes=8 << 20),
        cost_estimate=pl.CostEstimate(flops=0, bytes_accessed=1 << 17, transcendentals=0),
        name="publish",
    )(block)


def joined(core, mine, other, shape):
    return pl.pallas_call(
        join_kernel,
        out_shape=jax.ShapeDtypeStruct(shape, F32),
        in_specs=[SMEM, VMEM, VMEM],
        out_specs=pl.BlockSpec(memory_space=pl.ANY),
        scratch_shapes=[pltpu.SemaphoreType.DMA((2,))],
        compiler_params=pltpu.CompilerParams(vmem_limit_bytes=8 << 20),
        cost_estimate=pl.CostEstimate(flops=0, bytes_accessed=4 << 20, transcendentals=0),
        name="join",
    )(core.reshape(1), mine, other)


def exchange(block, axis):
    return lax.all_to_all(block, axis, split_axis=0, concat_axis=0, tiled=True)


def gather(block, axis):
    count = lax.axis_size(axis)
    return exchange(jnp.broadcast_to(block[None], (count, *block.shape)), axis)


def rotate(term, axis, step):
    count = lax.axis_size(axis)
    return lax.ppermute(term, axis, [(i, (i + step) % count) for i in range(count)])


def doubling(step):
    return [
        (2 * zhi + core, 2 * (zhi ^ 1 if core == step else 3 - zhi) + core)
        for zhi in range(4)
        for core in range(2)
    ]


def after(value, *others):
    return lax.optimization_barrier((value, *others))[0]


def shards(sizes, activations, weight, output_grad):
    _, zhis, rings, cores, spaces = sizes
    planes, height, lanes = activations.shape[1:]
    core = lax.axis_index("core")
    swap = [(0, 1), (1, 0)]

    outer = lax.ppermute(activations, AXES, neighbour(sizes, True, False))
    grads = [lax.ppermute(output_grad, AXES, neighbour(sizes, far, True)) for far in (False, True)]
    grad = jnp.concatenate(grads, axis=0)
    data = jnp.concatenate([activations, outer], axis=0)
    grad, data = lax.optimization_barrier((grad, data))
    data = gather(data, "space")
    grad = lax.all_gather(grad, "chan", axis=1, tiled=True)
    grad_inner = lax.ppermute(grad[0], "core", swap)

    keep, send, own = filter_partial(core, data, grad, grad_inner)
    moved = lax.ppermute(send, "core", swap)
    data_inner = lax.ppermute(after(own, send), "core", swap)
    half = small_call(add_kernel, keep.shape, keep, moved)
    half, data_inner = lax.optimization_barrier((half, data_inner))

    moved = exchange(half.reshape(rings, -1, lanes), "ring")
    me = lax.axis_index("space")
    back = convolve(True, core, me, after(grad, half), grad_inner, weight, spaces)
    back = [back[0], rotate(back[1], "space", 1), back[2], rotate(back[3], "space", 3)]
    quarter, *back = lax.optimization_barrier(
        (small_call(sum_kernel, moved.shape[1:], moved), *back)
    )

    moved = lax.ppermute(quarter, ("zhi", "core"), doubling(0))
    me = lax.axis_index("chan")
    forward = convolve(False, core, me, after(data, quarter), data_inner, weight, spaces)
    forward = [forward[0], rotate(forward[1], "chan", 1), *forward[2:]]
    cell_count = sizes[1] * rings * cores * grad.shape[1] * grad.shape[2]
    pair = quarter + moved
    pair, back, forward = lax.optimization_barrier((pair, back, forward))

    moved = lax.ppermute(pair, ("zhi", "core"), doubling(1))
    spread = functools.partial(spread_kernel, 1 / math.sqrt(cell_count))
    quarter = small_call(spread, (rings, *pair.shape), pair, moved)
    forward = [*forward[:2], rotate(forward[2], "chan", 2), rotate(forward[3], "chan", 3)]
    quarter, forward, back = lax.optimization_barrier((quarter, forward, back))

    half = exchange(quarter, "ring").reshape(-1, lanes)
    output = lax.ppermute(
        sum(forward).astype(BF16).reshape(activations.shape), AXES, neighbour(sizes, False, True)
    )
    output = published(output)
    back[2] = rotate(back[2], "space", 2)
    input_grad = sum(back).astype(BF16).reshape(activations.shape)
    half, _, _ = lax.optimization_barrier((half, output, input_grad))

    other = lax.ppermute(half, "core", swap)
    blocks = (-1, *weight.shape[1:])
    filter_grad = joined(core, half.reshape(blocks), other.reshape(blocks), weight.shape)
    return output, input_grad, filter_grad


def solution(mesh):
    chans, filts, spaces = (mesh.shape[name] for name in ("chan", "filt", "space"))
    sizes = (chans, filts // 8, 4, 2, spaces)
    fine = Mesh(mesh.devices.reshape(sizes), AXES)
    cells = P(("zhi", "ring", "core"), "space", None, "chan")
    filters = P(None, "chan", "space")
    return jax.shard_map(
        functools.partial(shards, sizes),
        mesh=fine,
        in_specs=(cells, filters, cells),
        out_specs=(cells, cells, filters),
        check_vma=False,
    )
```

```python
import functools
import math

import jax
import jax.numpy as jnp
import numpy as np
from jax import lax
from jax.experimental import pallas as pl
from jax.experimental.pallas import tpu as pltpu
from jax.sharding import Mesh, PartitionSpec as P

AXES = ("chan", "zhi", "ring", "core", "space")
F32 = jnp.float32
BF16 = jnp.bfloat16
VMEM = pl.BlockSpec(memory_space=pltpu.VMEM)
SMEM = pl.BlockSpec(memory_space=pltpu.SMEM)


def permutation(sizes, move):
    pairs = []
    for source in range(math.prod(sizes)):
        target = move(*(int(v) for v in np.unravel_index(source, sizes)))
        if target is not None:
            pairs.append((source, int(np.ravel_multi_index(target, sizes))))
    return pairs


def neighbour(sizes, outer, turn):
    _, zhis, rings, cores, _ = sizes

    def move(chan, zhi, ring, core, space):
        column = (zhi * rings + ring) * cores + core
        if outer:
            column += 1 if column % 2 else -1
        if not 0 <= column < zhis * rings * cores:
            return None
        if turn:
            chan, space = space, chan
        return (chan, column // (rings * cores), column // cores % rings, column % cores, space)

    return permutation(sizes, move)


def height_mask(rows, height, at):
    return lax.broadcasted_iota(jnp.int32, (rows, 128), 0) % height == at


def shifted(value, height, step):
    rows = value.shape[0]
    edge = 0 if step < 0 else height - 1
    rolled = pltpu.roll(value, (-step) % rows, 0)
    return jnp.where(height_mask(rows, height, edge), 0.0, rolled)


def fill_padded(padded, pair, inner, core):
    planes, height, lanes = padded.shape[1:]
    planes -= 2
    zero = jnp.zeros((3, 1, height, lanes), BF16)
    padded[:, 0:1] = zero
    padded[:, planes + 1 : planes + 2] = zero
    for column, source in ((1, 0), (2 * core, 1)):
        if len(pair.shape) == 4:
            padded[column, 1 : planes + 1] = pair[source]
        else:
            slabs, _, depth = pair.shape[:3]
            for slab in range(slabs):
                padded[column, 1 + slab * depth : 1 + (slab + 1) * depth] = pair[slab, source]
    padded[2 - 2 * core, 1 : planes + 1] = inner[...]


def conv_kernel(backward, place, pair, inner, weight, *refs):
    *outs, padded, flat = refs
    slabs = len(outs)
    rows, lanes = outs[0].shape
    height = inner.shape[1]
    planes = rows // height
    fill_padded(padded, pair, inner, place[0])
    for cell in range(9):
        for r in range(3):
            if backward:
                flat[r * lanes : (r + 1) * lanes, cell * lanes : (cell + 1) * lanes] = weight[3 * cell + r]
            else:
                flat[cell * lanes : (cell + 1) * lanes, r * lanes : (r + 1) * lanes] = weight[3 * cell + r]
    for step, out in enumerate(outs):
        slab = lax.rem(place[1] + step, slabs)
        pieces = []
        for p in range(3):
            for q in range(3):
                column, plane = (2 - p, 2 - q) if backward else (p, q)
                start = slab * planes + plane
                pieces.append(padded[column, pl.ds(start, planes)].reshape(rows, lanes))
        lhs = jnp.concatenate(pieces, axis=1)
        dims = (((1,), (1 if backward else 0,)), ((), ()))
        taps = lax.dot_general(lhs, flat[...], dims, preferred_element_type=F32)
        low, high = (2, 0) if backward else (0, 2)
        total = taps[:, lanes : 2 * lanes]
        total += shifted(taps[:, low * lanes : (low + 1) * lanes], height, -1)
        total += shifted(taps[:, high * lanes : (high + 1) * lanes], height, 1)
        out[...] = total


def convolve(backward, core, me, pair, inner, weight, slabs):
    planes, height, lanes = inner.shape
    rows = planes * height
    flat = (3 * lanes, 9 * lanes) if backward else (9 * lanes, 3 * lanes)
    return pl.pallas_call(
        functools.partial(conv_kernel, backward),
        out_shape=[jax.ShapeDtypeStruct((rows // slabs, lanes), F32)] * slabs,
        in_specs=[SMEM, VMEM, VMEM, VMEM],
        out_specs=[VMEM] * slabs,
        scratch_shapes=[
            pltpu.VMEM((3, planes + 2, height, lanes), BF16),
            pltpu.VMEM(flat, BF16),
        ],
        compiler_params=pltpu.CompilerParams(vmem_limit_bytes=14 << 20),
        cost_estimate=pl.CostEstimate(
            flops=2 * 27 * rows * lanes * lanes, bytes_accessed=3 << 20, transcendentals=0
        ),
        name="input_grad" if backward else "forward",
    )(jnp.stack([core, me]), pair, inner, weight)


def filter_kernel(core, data, pair, inner, keep, send, own, padded, turned, taps):
    planes, height, lanes = inner.shape
    rows = planes * height
    fill_padded(padded, pair, inner, core[0])
    own[...] = data[:, 0].reshape(own.shape)
    flat = data[:, 0].reshape(rows, lanes).astype(F32)
    turned[0:lanes] = shifted(flat, height, -1).T.astype(BF16)
    turned[lanes : 2 * lanes] = flat.T.astype(BF16)
    turned[2 * lanes : 3 * lanes] = shifted(flat, height, 1).T.astype(BF16)
    for p in range(3):
        pieces = [padded[2 - p, 2 - q : 2 - q + planes].reshape(rows, lanes) for q in range(3)]
        rhs = jnp.concatenate(pieces, axis=1)
        result = jnp.dot(turned[...], rhs, preferred_element_type=F32)
        for q in range(3):
            for r in range(3):
                tap = 9 * p + 3 * q + r
                taps[tap * lanes : (tap + 1) * lanes] = result[
                    r * lanes : (r + 1) * lanes, q * lanes : (q + 1) * lanes
                ]
    taps[27 * lanes :] = jnp.zeros((lanes, lanes), F32)
    half = keep.shape[0]

    @pl.when(core[0] == 0)
    def _():
        keep[...] = taps[0:half]
        send[...] = taps[half : 2 * half]

    @pl.when(core[0] == 1)
    def _():
        keep[...] = taps[half : 2 * half]
        send[...] = taps[0:half]


def filter_partial(core, data, pair, inner):
    planes, height, lanes = inner.shape
    rows = planes * height
    half = jax.ShapeDtypeStruct((14 * lanes, lanes), F32)
    return pl.pallas_call(
        filter_kernel,
        out_shape=(half, half, jax.ShapeDtypeStruct(inner.shape, BF16)),
        in_specs=[SMEM, VMEM, VMEM, VMEM],
        out_specs=(VMEM, VMEM, VMEM),
        scratch_shapes=[
            pltpu.VMEM((3, planes + 2, height, lanes), BF16),
            pltpu.VMEM((3 * lanes, rows), BF16),
            pltpu.VMEM((28 * lanes, lanes), F32),
        ],
        compiler_params=pltpu.CompilerParams(vmem_limit_bytes=14 << 20),
        cost_estimate=pl.CostEstimate(
            flops=2 * 27 * rows * lanes * lanes, bytes_accessed=3 << 20, transcendentals=0
        ),
        name="filter_grad",
    )(core.reshape(1), data, pair, inner)


def small_call(kernel, shape, *operands):
    return pl.pallas_call(
        kernel,
        out_shape=jax.ShapeDtypeStruct(shape, F32),
        in_specs=[VMEM] * len(operands),
        out_specs=VMEM,
        compiler_params=pltpu.CompilerParams(vmem_limit_bytes=8 << 20),
        cost_estimate=pl.CostEstimate(
            flops=operands[0].size, bytes_accessed=1 << 20, transcendentals=0
        ),
    )(*operands)


def add_kernel(left, right, out):
    out[...] = left[...] + right[...]


def sum_kernel(parts, out):
    out[...] = (parts[0] + parts[1]) + (parts[2] + parts[3])


def spread_kernel(scale, left, right, out):
    total = (left[...] + right[...]) * scale
    for copy in range(out.shape[0]):
        out[copy] = total


def join_kernel(core, mine, other, out, sems):
    size, rest = mine.shape[0], out.shape[0] - mine.shape[0]

    def place(low, high):
        copies = [
            pltpu.make_async_copy(low, out.at[pl.ds(0, size)], sems.at[0]),
            pltpu.make_async_copy(high.at[pl.ds(0, rest)], out.at[pl.ds(size, rest)], sems.at[1]),
        ]
        for copy in copies:
            copy.start()
        for copy in copies:
            copy.wait()

    @pl.when(core[0] == 0)
    def _():
        place(mine, other)

    @pl.when(core[0] == 1)
    def _():
        place(other, mine)


def copy_kernel(block, out):
    out[...] = block[...]


def published(block):
    return pl.pallas_call(
        copy_kernel,
        out_shape=jax.ShapeDtypeStruct(block.shape, block.dtype),
        in_specs=[VMEM],
        out_specs=VMEM,
        compiler_params=pltpu.CompilerParams(vmem_limit_bytes=8 << 20),
        cost_estimate=pl.CostEstimate(flops=0, bytes_accessed=1 << 17, transcendentals=0),
        name="publish",
    )(block)


def joined(core, mine, other, shape):
    return pl.pallas_call(
        join_kernel,
        out_shape=jax.ShapeDtypeStruct(shape, F32),
        in_specs=[SMEM, VMEM, VMEM],
        out_specs=pl.BlockSpec(memory_space=pl.ANY),
        scratch_shapes=[pltpu.SemaphoreType.DMA((2,))],
        compiler_params=pltpu.CompilerParams(vmem_limit_bytes=8 << 20),
        cost_estimate=pl.CostEstimate(flops=0, bytes_accessed=4 << 20, transcendentals=0),
        name="join",
    )(core.reshape(1), mine, other)


def exchange(block, axis):
    return lax.all_to_all(block, axis, split_axis=0, concat_axis=0, tiled=True)


def rotate(term, axis, step):
    count = lax.axis_size(axis)
    return lax.ppermute(term, axis, [(i, (i + step) % count) for i in range(count)])


def doubling(step):
    return [
        (2 * zhi + core, 2 * (zhi ^ 1 if core == step else 3 - zhi) + core)
        for zhi in range(4)
        for core in range(2)
    ]


def after(value, *others):
    return lax.optimization_barrier((value, *others))[0]


def shards(sizes, activations, weight, output_grad):
    chans, _, rings, cores, spaces = sizes
    planes, height, lanes = activations.shape[1:]
    core = lax.axis_index("core")
    swap = [(0, 1), (1, 0)]

    outer = lax.ppermute(activations, AXES, neighbour(sizes, True, False))
    grads = [lax.ppermute(output_grad, AXES, neighbour(sizes, far, True)) for far in (False, True)]
    grad = jnp.concatenate(grads, axis=0)
    data = jnp.concatenate([activations, outer], axis=0)
    data = jnp.broadcast_to(data[None], (spaces, *data.shape))
    grad, data = lax.optimization_barrier((grad, data))
    data = exchange(data, "space")
    grad = lax.all_gather(grad, "chan", axis=1, tiled=True)
    grad_inner = lax.ppermute(grad[0], "core", swap)

    keep, send, own = filter_partial(core, data, grad, grad_inner)
    moved = lax.ppermute(send, "core", swap)
    data_inner = lax.ppermute(after(own, send), "core", swap)
    half = small_call(add_kernel, keep.shape, keep, moved)
    half, data_inner = lax.optimization_barrier((half, data_inner))

    moved = exchange(half.reshape(rings, -1, lanes), "ring")
    me = lax.axis_index("space")
    back = convolve(True, core, me, after(grad, half), grad_inner, weight, spaces)
    back = [back[0], rotate(back[1], "space", 1), back[2], rotate(back[3], "space", 3)]
    quarter, *back = lax.optimization_barrier(
        (small_call(sum_kernel, moved.shape[1:], moved), *back)
    )

    moved = lax.ppermute(quarter, ("zhi", "core"), doubling(0))
    me = lax.axis_index("chan")
    forward = convolve(False, core, me, after(data, quarter), data_inner, weight, spaces)
    forward = [forward[0], *(rotate(forward[step], "chan", step) for step in range(1, chans))]
    cell_count = sizes[1] * rings * cores * grad.shape[1] * grad.shape[2]
    pair = quarter + moved
    pair, back, forward = lax.optimization_barrier((pair, back, forward))

    moved = lax.ppermute(pair, ("zhi", "core"), doubling(1))
    spread = functools.partial(spread_kernel, 1 / math.sqrt(cell_count))
    quarter = small_call(spread, (rings, *pair.shape), pair, moved)
    forward = sum(forward).astype(BF16).reshape(activations.shape)
    output = published(lax.ppermute(forward, AXES, neighbour(sizes, False, True)))
    quarter, output, back = lax.optimization_barrier((quarter, output, back))

    half = exchange(quarter, "ring").reshape(-1, lanes)
    back[2] = rotate(back[2], "space", 2)
    input_grad = sum(back).astype(BF16).reshape(activations.shape)
    half = after(half, input_grad)

    other = lax.ppermute(half, "core", swap)
    blocks = (-1, *weight.shape[1:])
    filter_grad = joined(core, half.reshape(blocks), other.reshape(blocks), weight.shape)
    return output, input_grad, filter_grad


def solution(mesh):
    chans, filts, spaces = (mesh.shape[name] for name in ("chan", "filt", "space"))
    sizes = (chans, filts // 8, 4, 2, spaces)
    fine = Mesh(mesh.devices.reshape(sizes), AXES)
    cells = P(("zhi", "ring", "core"), "space", None, "chan")
    filters = P(None, "chan", "space")
    return jax.shard_map(
        functools.partial(shards, sizes),
        mesh=fine,
        in_specs=(cells, filters, cells),
        out_specs=(cells, cells, filters),
        check_vma=False,
    )
```

```python
import functools
import math

import jax
import jax.numpy as jnp
import numpy as np
from jax import lax
from jax.experimental import pallas as pl
from jax.experimental.pallas import tpu as pltpu
from jax.sharding import Mesh, PartitionSpec as P

AXES = ("chan", "zhi", "ring", "core", "space")
F32 = jnp.float32
BF16 = jnp.bfloat16
VMEM = pl.BlockSpec(memory_space=pltpu.VMEM)
SMEM = pl.BlockSpec(memory_space=pltpu.SMEM)


def permutation(sizes, move):
    pairs = []
    for source in range(math.prod(sizes)):
        target = move(*(int(v) for v in np.unravel_index(source, sizes)))
        if target is not None:
            pairs.append((source, int(np.ravel_multi_index(target, sizes))))
    return pairs


def neighbour(sizes, outer, turn):
    _, zhis, rings, cores, _ = sizes

    def move(chan, zhi, ring, core, space):
        column = (zhi * rings + ring) * cores + core
        if outer:
            column += 1 if column % 2 else -1
        if not 0 <= column < zhis * rings * cores:
            return None
        if turn:
            chan, space = space, chan
        return (chan, column // (rings * cores), column // cores % rings, column % cores, space)

    return permutation(sizes, move)


def height_mask(rows, height, at):
    return lax.broadcasted_iota(jnp.int32, (rows, 128), 0) % height == at


def shifted(value, height, step):
    rows = value.shape[0]
    edge = 0 if step < 0 else height - 1
    rolled = pltpu.roll(value, (-step) % rows, 0)
    return jnp.where(height_mask(rows, height, edge), 0.0, rolled)


def fill_padded(padded, pair, inner, core):
    planes, height, lanes = padded.shape[1:]
    planes -= 2
    zero = jnp.zeros((3, 1, height, lanes), BF16)
    padded[:, 0:1] = zero
    padded[:, planes + 1 : planes + 2] = zero
    for column, source in ((1, 0), (2 * core, 1)):
        if len(pair.shape) == 4:
            padded[column, 1 : planes + 1] = pair[source]
        else:
            slabs, _, depth = pair.shape[:3]
            for slab in range(slabs):
                padded[column, 1 + slab * depth : 1 + (slab + 1) * depth] = pair[slab, source]
    padded[2 - 2 * core, 1 : planes + 1] = inner[...]


def conv_kernel(backward, place, pair, inner, weight, *refs):
    *outs, padded, flat = refs
    slabs = len(outs)
    rows, lanes = outs[0].shape
    height = inner.shape[1]
    planes = rows // height
    fill_padded(padded, pair, inner, place[0])
    for cell in range(9):
        for r in range(3):
            if backward:
                flat[r * lanes : (r + 1) * lanes, cell * lanes : (cell + 1) * lanes] = weight[3 * cell + r]
            else:
                flat[cell * lanes : (cell + 1) * lanes, r * lanes : (r + 1) * lanes] = weight[3 * cell + r]
    for step, out in enumerate(outs):
        slab = lax.rem(place[1] + step, slabs)
        pieces = []
        for p in range(3):
            for q in range(3):
                column, plane = (2 - p, 2 - q) if backward else (p, q)
                start = slab * planes + plane
                pieces.append(padded[column, pl.ds(start, planes)].reshape(rows, lanes))
        lhs = jnp.concatenate(pieces, axis=1)
        dims = (((1,), (1 if backward else 0,)), ((), ()))
        taps = lax.dot_general(lhs, flat[...], dims, preferred_element_type=F32)
        low, high = (2, 0) if backward else (0, 2)
        total = taps[:, lanes : 2 * lanes]
        total += shifted(taps[:, low * lanes : (low + 1) * lanes], height, -1)
        total += shifted(taps[:, high * lanes : (high + 1) * lanes], height, 1)
        out[...] = total


def convolve(backward, core, me, pair, inner, weight, slabs):
    planes, height, lanes = inner.shape
    rows = planes * height
    flat = (3 * lanes, 9 * lanes) if backward else (9 * lanes, 3 * lanes)
    return pl.pallas_call(
        functools.partial(conv_kernel, backward),
        out_shape=[jax.ShapeDtypeStruct((rows // slabs, lanes), F32)] * slabs,
        in_specs=[SMEM, VMEM, VMEM, VMEM],
        out_specs=[VMEM] * slabs,
        scratch_shapes=[
            pltpu.VMEM((3, planes + 2, height, lanes), BF16),
            pltpu.VMEM(flat, BF16),
        ],
        compiler_params=pltpu.CompilerParams(vmem_limit_bytes=14 << 20),
        cost_estimate=pl.CostEstimate(
            flops=2 * 27 * rows * lanes * lanes, bytes_accessed=3 << 20, transcendentals=0
        ),
        name="input_grad" if backward else "forward",
    )(jnp.stack([core, me]), pair, inner, weight)


def filter_kernel(core, data, pair, inner, keep, send, own, padded, turned, taps):
    planes, height, lanes = inner.shape
    rows = planes * height
    fill_padded(padded, pair, inner, core[0])
    own[...] = data[:, 0].reshape(own.shape)
    flat = data[:, 0].reshape(rows, lanes).astype(F32)
    turned[0:lanes] = shifted(flat, height, -1).T.astype(BF16)
    turned[lanes : 2 * lanes] = flat.T.astype(BF16)
    turned[2 * lanes : 3 * lanes] = shifted(flat, height, 1).T.astype(BF16)
    for p in range(3):
        pieces = [padded[2 - p, 2 - q : 2 - q + planes].reshape(rows, lanes) for q in range(3)]
        rhs = jnp.concatenate(pieces, axis=1)
        result = jnp.dot(turned[...], rhs, preferred_element_type=F32)
        for q in range(3):
            for r in range(3):
                tap = 9 * p + 3 * q + r
                taps[tap * lanes : (tap + 1) * lanes] = result[
                    r * lanes : (r + 1) * lanes, q * lanes : (q + 1) * lanes
                ]
    taps[27 * lanes :] = jnp.zeros((lanes, lanes), F32)
    half = keep.shape[0]

    @pl.when(core[0] == 0)
    def _():
        keep[...] = taps[0:half]
        send[...] = taps[half : 2 * half]

    @pl.when(core[0] == 1)
    def _():
        keep[...] = taps[half : 2 * half]
        send[...] = taps[0:half]


def filter_partial(core, data, pair, inner):
    planes, height, lanes = inner.shape
    rows = planes * height
    half = jax.ShapeDtypeStruct((14 * lanes, lanes), F32)
    return pl.pallas_call(
        filter_kernel,
        out_shape=(half, half, jax.ShapeDtypeStruct(inner.shape, BF16)),
        in_specs=[SMEM, VMEM, VMEM, VMEM],
        out_specs=(VMEM, VMEM, VMEM),
        scratch_shapes=[
            pltpu.VMEM((3, planes + 2, height, lanes), BF16),
            pltpu.VMEM((3 * lanes, rows), BF16),
            pltpu.VMEM((28 * lanes, lanes), F32),
        ],
        compiler_params=pltpu.CompilerParams(vmem_limit_bytes=14 << 20),
        cost_estimate=pl.CostEstimate(
            flops=2 * 27 * rows * lanes * lanes, bytes_accessed=3 << 20, transcendentals=0
        ),
        name="filter_grad",
    )(core.reshape(1), data, pair, inner)


def small_call(kernel, shape, *operands):
    return pl.pallas_call(
        kernel,
        out_shape=jax.ShapeDtypeStruct(shape, F32),
        in_specs=[VMEM] * len(operands),
        out_specs=VMEM,
        compiler_params=pltpu.CompilerParams(vmem_limit_bytes=8 << 20),
        cost_estimate=pl.CostEstimate(
            flops=operands[0].size, bytes_accessed=1 << 20, transcendentals=0
        ),
    )(*operands)


def add_kernel(left, right, out):
    out[...] = left[...] + right[...]


def sum_kernel(parts, out):
    out[...] = (parts[0] + parts[1]) + (parts[2] + parts[3])


def spread_kernel(scale, left, right, out):
    total = (left[...] + right[...]) * scale
    for copy in range(out.shape[0]):
        out[copy] = total


def join_kernel(core, mine, other, out, sems):
    size, rest = mine.shape[0], out.shape[0] - mine.shape[0]

    def place(low, high):
        copies = [
            pltpu.make_async_copy(low, out.at[pl.ds(0, size)], sems.at[0]),
            pltpu.make_async_copy(high.at[pl.ds(0, rest)], out.at[pl.ds(size, rest)], sems.at[1]),
        ]
        for copy in copies:
            copy.start()
        for copy in copies:
            copy.wait()

    @pl.when(core[0] == 0)
    def _():
        place(mine, other)

    @pl.when(core[0] == 1)
    def _():
        place(other, mine)


def copy_kernel(block, out):
    out[...] = block[...]


def published(block):
    return pl.pallas_call(
        copy_kernel,
        out_shape=jax.ShapeDtypeStruct(block.shape, block.dtype),
        in_specs=[VMEM],
        out_specs=VMEM,
        compiler_params=pltpu.CompilerParams(vmem_limit_bytes=8 << 20),
        cost_estimate=pl.CostEstimate(flops=0, bytes_accessed=1 << 17, transcendentals=0),
        name="publish",
    )(block)


def joined(core, mine, other, shape):
    return pl.pallas_call(
        join_kernel,
        out_shape=jax.ShapeDtypeStruct(shape, F32),
        in_specs=[SMEM, VMEM, VMEM],
        out_specs=pl.BlockSpec(memory_space=pl.ANY),
        scratch_shapes=[pltpu.SemaphoreType.DMA((2,))],
        compiler_params=pltpu.CompilerParams(vmem_limit_bytes=8 << 20),
        cost_estimate=pl.CostEstimate(flops=0, bytes_accessed=4 << 20, transcendentals=0),
        name="join",
    )(core.reshape(1), mine, other)


def exchange(block, axis):
    return lax.all_to_all(block, axis, split_axis=0, concat_axis=0, tiled=True)


def rotate(term, axis, step):
    count = lax.axis_size(axis)
    return lax.ppermute(term, axis, [(i, (i + step) % count) for i in range(count)])


def doubling(step):
    return [
        (2 * zhi + core, 2 * (zhi ^ 1 if core == step else 3 - zhi) + core)
        for zhi in range(4)
        for core in range(2)
    ]


def after(value, *others):
    return lax.optimization_barrier((value, *others))[0]


def shards(sizes, activations, weight, output_grad):
    _, _, rings, cores, spaces = sizes
    planes, height, lanes = activations.shape[1:]
    core = lax.axis_index("core")
    swap = [(0, 1), (1, 0)]

    outer = lax.ppermute(activations, AXES, neighbour(sizes, True, False))
    grads = [lax.ppermute(output_grad, AXES, neighbour(sizes, far, True)) for far in (False, True)]
    grad = jnp.concatenate(grads, axis=0)
    data = jnp.concatenate([activations, outer], axis=0)
    data = jnp.broadcast_to(data[None], (spaces, *data.shape))
    grad, data = lax.optimization_barrier((grad, data))
    data = exchange(data, "space")
    grad = lax.all_gather(grad, "chan", axis=1, tiled=True)
    grad_inner = lax.ppermute(grad[0], "core", swap)

    keep, send, own = filter_partial(core, data, grad, grad_inner)
    moved = lax.ppermute(send, "core", swap)
    data_inner = lax.ppermute(after(own, send), "core", swap)
    half = small_call(add_kernel, keep.shape, keep, moved)
    half, data_inner = lax.optimization_barrier((half, data_inner))

    moved = exchange(half.reshape(rings, -1, lanes), "ring")
    me = lax.axis_index("space")
    back = convolve(True, core, me, after(grad, half), grad_inner, weight, spaces)
    back = [back[0], rotate(back[1], "space", 1), back[2], rotate(back[3], "space", 3)]
    quarter, *back = lax.optimization_barrier(
        (small_call(sum_kernel, moved.shape[1:], moved), *back)
    )

    moved = lax.ppermute(quarter, ("zhi", "core"), doubling(0))
    me = lax.axis_index("chan")
    forward = convolve(False, core, me, after(data, quarter), data_inner, weight, spaces)
    forward = [forward[0], rotate(forward[1], "chan", 1), rotate(forward[2], "chan", 2), forward[3]]
    cell_count = sizes[1] * rings * cores * grad.shape[1] * grad.shape[2]
    pair = quarter + moved
    pair, back, forward = lax.optimization_barrier((pair, back, forward))

    moved = lax.ppermute(pair, ("zhi", "core"), doubling(1))
    spread = functools.partial(spread_kernel, 1 / math.sqrt(cell_count))
    quarter = small_call(spread, (rings, *pair.shape), pair, moved)
    forward[3] = rotate(forward[3], "chan", 3)
    quarter, forward, back = lax.optimization_barrier((quarter, forward, back))

    half = exchange(quarter, "ring").reshape(-1, lanes)
    forward = sum(forward).astype(BF16).reshape(activations.shape)
    output = published(lax.ppermute(forward, AXES, neighbour(sizes, False, True)))
    back[2] = rotate(after(back[2], forward), "space", 2)
    half, _, back = lax.optimization_barrier((half, output, back))
    input_grad = sum(back).astype(BF16).reshape(activations.shape)

    other = lax.ppermute(half, "core", swap)
    blocks = (-1, *weight.shape[1:])
    filter_grad = joined(core, half.reshape(blocks), other.reshape(blocks), weight.shape)
    return output, input_grad, filter_grad


def solution(mesh):
    chans, filts, spaces = (mesh.shape[name] for name in ("chan", "filt", "space"))
    sizes = (chans, filts // 8, 4, 2, spaces)
    fine = Mesh(mesh.devices.reshape(sizes), AXES)
    cells = P(("zhi", "ring", "core"), "space", None, "chan")
    filters = P(None, "chan", "space")
    return jax.shard_map(
        functools.partial(shards, sizes),
        mesh=fine,
        in_specs=(cells, filters, cells),
        out_specs=(cells, cells, filters),
        check_vma=False,
    )
```

```python
import functools
import math

import jax
import jax.numpy as jnp
import numpy as np
from jax import lax
from jax.experimental import pallas as pl
from jax.experimental.pallas import tpu as pltpu
from jax.sharding import Mesh, PartitionSpec as P

AXES = ("chan", "zhi", "ring", "core", "space")
F32 = jnp.float32
BF16 = jnp.bfloat16
VMEM = pl.BlockSpec(memory_space=pltpu.VMEM)
SMEM = pl.BlockSpec(memory_space=pltpu.SMEM)


def permutation(sizes, move):
    pairs = []
    for source in range(math.prod(sizes)):
        target = move(*(int(v) for v in np.unravel_index(source, sizes)))
        if target is not None:
            pairs.append((source, int(np.ravel_multi_index(target, sizes))))
    return pairs


def neighbour(sizes, outer, turn):
    _, zhis, rings, cores, _ = sizes

    def move(chan, zhi, ring, core, space):
        column = (zhi * rings + ring) * cores + core
        if outer:
            column += 1 if column % 2 else -1
        if not 0 <= column < zhis * rings * cores:
            return None
        if turn:
            chan, space = space, chan
        return (chan, column // (rings * cores), column // cores % rings, column % cores, space)

    return permutation(sizes, move)


def height_mask(rows, height, at):
    return lax.broadcasted_iota(jnp.int32, (rows, 128), 0) % height == at


def shifted(value, height, step):
    rows = value.shape[0]
    edge = 0 if step < 0 else height - 1
    rolled = pltpu.roll(value, (-step) % rows, 0)
    return jnp.where(height_mask(rows, height, edge), 0.0, rolled)


def fill_padded(padded, pair, inner, core):
    planes, height, lanes = padded.shape[1:]
    planes -= 2
    zero = jnp.zeros((3, 1, height, lanes), BF16)
    padded[:, 0:1] = zero
    padded[:, planes + 1 : planes + 2] = zero
    for column, source in ((1, 0), (2 * core, 1)):
        if len(pair.shape) == 4:
            padded[column, 1 : planes + 1] = pair[source]
        else:
            slabs, _, depth = pair.shape[:3]
            for slab in range(slabs):
                padded[column, 1 + slab * depth : 1 + (slab + 1) * depth] = pair[slab, source]
    padded[2 - 2 * core, 1 : planes + 1] = inner[...]


def conv_kernel(backward, place, pair, inner, weight, *refs):
    *outs, padded, flat = refs
    slabs = len(outs)
    rows, lanes = outs[0].shape
    height = inner.shape[1]
    planes = rows // height
    fill_padded(padded, pair, inner, place[0])
    for cell in range(9):
        for r in range(3):
            if backward:
                flat[r * lanes : (r + 1) * lanes, cell * lanes : (cell + 1) * lanes] = weight[3 * cell + r]
            else:
                flat[cell * lanes : (cell + 1) * lanes, r * lanes : (r + 1) * lanes] = weight[3 * cell + r]
    for step, out in enumerate(outs):
        slab = lax.rem(place[1] + step, slabs)
        pieces = []
        for p in range(3):
            for q in range(3):
                column, plane = (2 - p, 2 - q) if backward else (p, q)
                start = slab * planes + plane
                pieces.append(padded[column, pl.ds(start, planes)].reshape(rows, lanes))
        lhs = jnp.concatenate(pieces, axis=1)
        dims = (((1,), (1 if backward else 0,)), ((), ()))
        taps = lax.dot_general(lhs, flat[...], dims, preferred_element_type=F32)
        low, high = (2, 0) if backward else (0, 2)
        total = taps[:, lanes : 2 * lanes]
        total += shifted(taps[:, low * lanes : (low + 1) * lanes], height, -1)
        total += shifted(taps[:, high * lanes : (high + 1) * lanes], height, 1)
        out[...] = total


def convolve(backward, core, me, pair, inner, weight, slabs):
    planes, height, lanes = inner.shape
    rows = planes * height
    flat = (3 * lanes, 9 * lanes) if backward else (9 * lanes, 3 * lanes)
    return pl.pallas_call(
        functools.partial(conv_kernel, backward),
        out_shape=[jax.ShapeDtypeStruct((rows // slabs, lanes), F32)] * slabs,
        in_specs=[SMEM, VMEM, VMEM, VMEM],
        out_specs=[VMEM] * slabs,
        scratch_shapes=[
            pltpu.VMEM((3, planes + 2, height, lanes), BF16),
            pltpu.VMEM(flat, BF16),
        ],
        compiler_params=pltpu.CompilerParams(vmem_limit_bytes=14 << 20),
        cost_estimate=pl.CostEstimate(
            flops=2 * 27 * rows * lanes * lanes, bytes_accessed=3 << 20, transcendentals=0
        ),
        name="input_grad" if backward else "forward",
    )(jnp.stack([core, me]), pair, inner, weight)


def filter_kernel(core, data, pair, inner, keep, send, own, padded, turned, taps):
    planes, height, lanes = inner.shape
    rows = planes * height
    fill_padded(padded, pair, inner, core[0])
    own[...] = data[:, 0].reshape(own.shape)
    flat = data[:, 0].reshape(rows, lanes).astype(F32)
    turned[0:lanes] = shifted(flat, height, -1).T.astype(BF16)
    turned[lanes : 2 * lanes] = flat.T.astype(BF16)
    turned[2 * lanes : 3 * lanes] = shifted(flat, height, 1).T.astype(BF16)
    for p in range(3):
        pieces = [padded[2 - p, 2 - q : 2 - q + planes].reshape(rows, lanes) for q in range(3)]
        rhs = jnp.concatenate(pieces, axis=1)
        result = jnp.dot(turned[...], rhs, preferred_element_type=F32)
        for q in range(3):
            for r in range(3):
                tap = 9 * p + 3 * q + r
                taps[tap * lanes : (tap + 1) * lanes] = result[
                    r * lanes : (r + 1) * lanes, q * lanes : (q + 1) * lanes
                ]
    taps[27 * lanes :] = jnp.zeros((lanes, lanes), F32)
    half = keep.shape[0]

    @pl.when(core[0] == 0)
    def _():
        keep[...] = taps[0:half]
        send[...] = taps[half : 2 * half]

    @pl.when(core[0] == 1)
    def _():
        keep[...] = taps[half : 2 * half]
        send[...] = taps[0:half]


def filter_partial(core, data, pair, inner):
    planes, height, lanes = inner.shape
    rows = planes * height
    half = jax.ShapeDtypeStruct((14 * lanes, lanes), F32)
    return pl.pallas_call(
        filter_kernel,
        out_shape=(half, half, jax.ShapeDtypeStruct(inner.shape, BF16)),
        in_specs=[SMEM, VMEM, VMEM, VMEM],
        out_specs=(VMEM, VMEM, VMEM),
        scratch_shapes=[
            pltpu.VMEM((3, planes + 2, height, lanes), BF16),
            pltpu.VMEM((3 * lanes, rows), BF16),
            pltpu.VMEM((28 * lanes, lanes), F32),
        ],
        compiler_params=pltpu.CompilerParams(vmem_limit_bytes=14 << 20),
        cost_estimate=pl.CostEstimate(
            flops=2 * 27 * rows * lanes * lanes, bytes_accessed=3 << 20, transcendentals=0
        ),
        name="filter_grad",
    )(core.reshape(1), data, pair, inner)


def small_call(kernel, shape, *operands):
    return pl.pallas_call(
        kernel,
        out_shape=jax.ShapeDtypeStruct(shape, F32),
        in_specs=[VMEM] * len(operands),
        out_specs=VMEM,
        compiler_params=pltpu.CompilerParams(vmem_limit_bytes=8 << 20),
        cost_estimate=pl.CostEstimate(
            flops=operands[0].size, bytes_accessed=1 << 20, transcendentals=0
        ),
    )(*operands)


def add_kernel(left, right, out):
    out[...] = left[...] + right[...]


def sum_kernel(parts, out):
    out[...] = (parts[0] + parts[1]) + (parts[2] + parts[3])


def spread_kernel(scale, left, right, out):
    total = (left[...] + right[...]) * scale
    for copy in range(out.shape[0]):
        out[copy] = total


def join_kernel(core, mine, other, out, sems):
    size, rest = mine.shape[0], out.shape[0] - mine.shape[0]

    def place(low, high):
        copies = [
            pltpu.make_async_copy(low, out.at[pl.ds(0, size)], sems.at[0]),
            pltpu.make_async_copy(high.at[pl.ds(0, rest)], out.at[pl.ds(size, rest)], sems.at[1]),
        ]
        for copy in copies:
            copy.start()
        for copy in copies:
            copy.wait()

    @pl.when(core[0] == 0)
    def _():
        place(mine, other)

    @pl.when(core[0] == 1)
    def _():
        place(other, mine)


def copy_kernel(block, out):
    out[...] = block[...]


def published(block):
    return pl.pallas_call(
        copy_kernel,
        out_shape=jax.ShapeDtypeStruct(block.shape, block.dtype),
        in_specs=[VMEM],
        out_specs=VMEM,
        compiler_params=pltpu.CompilerParams(vmem_limit_bytes=8 << 20),
        cost_estimate=pl.CostEstimate(flops=0, bytes_accessed=1 << 17, transcendentals=0),
        name="publish",
    )(block)


def pack_kernel(own, outer, out):
    for copy in range(out.shape[0]):
        out[copy, 0:1] = own[...]
        out[copy, 1:2] = outer[...]


def packed(own, outer, copies):
    return pl.pallas_call(
        pack_kernel,
        out_shape=jax.ShapeDtypeStruct((copies, 2, *own.shape[1:]), own.dtype),
        in_specs=[VMEM, VMEM],
        out_specs=VMEM,
        compiler_params=pltpu.CompilerParams(vmem_limit_bytes=8 << 20),
        cost_estimate=pl.CostEstimate(flops=0, bytes_accessed=1 << 19, transcendentals=0),
        name="pack",
    )(own, outer)


def joined(core, mine, other, shape):
    return pl.pallas_call(
        join_kernel,
        out_shape=jax.ShapeDtypeStruct(shape, F32),
        in_specs=[SMEM, VMEM, VMEM],
        out_specs=pl.BlockSpec(memory_space=pl.ANY),
        scratch_shapes=[pltpu.SemaphoreType.DMA((2,))],
        compiler_params=pltpu.CompilerParams(vmem_limit_bytes=8 << 20),
        cost_estimate=pl.CostEstimate(flops=0, bytes_accessed=4 << 20, transcendentals=0),
        name="join",
    )(core.reshape(1), mine, other)


def exchange(block, axis):
    return lax.all_to_all(block, axis, split_axis=0, concat_axis=0, tiled=True)


def rotate(term, axis, step):
    count = lax.axis_size(axis)
    return lax.ppermute(term, axis, [(i, (i + step) % count) for i in range(count)])


def doubling(step):
    return [
        (2 * zhi + core, 2 * (zhi ^ 1 if core == step else 3 - zhi) + core)
        for zhi in range(4)
        for core in range(2)
    ]


def after(value, *others):
    return lax.optimization_barrier((value, *others))[0]


def shards(sizes, activations, weight, output_grad):
    _, _, rings, cores, spaces = sizes
    planes, height, lanes = activations.shape[1:]
    core = lax.axis_index("core")
    swap = [(0, 1), (1, 0)]

    outer = lax.ppermute(activations, AXES, neighbour(sizes, True, False))
    grads = [lax.ppermute(output_grad, AXES, neighbour(sizes, far, True)) for far in (False, True)]
    grad = jnp.concatenate(grads, axis=0)
    grad, outer = lax.optimization_barrier((grad, outer))
    data = exchange(packed(activations, outer, spaces), "space")
    grad = lax.all_gather(grad, "chan", axis=1, tiled=True)
    grad_inner = lax.ppermute(grad[0], "core", swap)

    keep, send, own = filter_partial(core, data, grad, grad_inner)
    moved = lax.ppermute(send, "core", swap)
    data_inner = lax.ppermute(after(own, send), "core", swap)
    half = small_call(add_kernel, keep.shape, keep, moved)
    half, data_inner = lax.optimization_barrier((half, data_inner))

    moved = exchange(half.reshape(rings, -1, lanes), "ring")
    me = lax.axis_index("space")
    back = convolve(True, core, me, after(grad, half), grad_inner, weight, spaces)
    back = [back[0], rotate(back[1], "space", 1), back[2], rotate(back[3], "space", 3)]
    quarter, *back = lax.optimization_barrier(
        (small_call(sum_kernel, moved.shape[1:], moved), *back)
    )

    moved = lax.ppermute(quarter, ("zhi", "core"), doubling(0))
    me = lax.axis_index("chan")
    forward = convolve(False, core, me, after(data, quarter), data_inner, weight, spaces)
    forward = [forward[0], rotate(forward[1], "chan", 1), rotate(forward[2], "chan", 2), forward[3]]
    cell_count = sizes[1] * rings * cores * grad.shape[1] * grad.shape[2]
    pair = quarter + moved
    pair, back, forward = lax.optimization_barrier((pair, back, forward))

    moved = lax.ppermute(pair, ("zhi", "core"), doubling(1))
    spread = functools.partial(spread_kernel, 1 / math.sqrt(cell_count))
    quarter = small_call(spread, (rings, *pair.shape), pair, moved)
    forward[3] = rotate(forward[3], "chan", 3)
    quarter, forward, back = lax.optimization_barrier((quarter, forward, back))

    half = exchange(quarter, "ring").reshape(-1, lanes)
    forward = sum(forward).astype(BF16).reshape(activations.shape)
    output = published(lax.ppermute(forward, AXES, neighbour(sizes, False, True)))
    back[2] = rotate(after(back[2], forward), "space", 2)
    half, _, back = lax.optimization_barrier((half, output, back))
    input_grad = sum(back).astype(BF16).reshape(activations.shape)

    other = lax.ppermute(half, "core", swap)
    blocks = (-1, *weight.shape[1:])
    filter_grad = joined(core, half.reshape(blocks), other.reshape(blocks), weight.shape)
    return output, input_grad, filter_grad


def solution(mesh):
    chans, filts, spaces = (mesh.shape[name] for name in ("chan", "filt", "space"))
    sizes = (chans, filts // 8, 4, 2, spaces)
    fine = Mesh(mesh.devices.reshape(sizes), AXES)
    cells = P(("zhi", "ring", "core"), "space", None, "chan")
    filters = P(None, "chan", "space")
    return jax.shard_map(
        functools.partial(shards, sizes),
        mesh=fine,
        in_specs=(cells, filters, cells),
        out_specs=(cells, cells, filters),
        check_vma=False,
    )
```

```python
import functools
import math

import jax
import jax.numpy as jnp
import numpy as np
from jax import lax
from jax.experimental import pallas as pl
from jax.experimental.pallas import tpu as pltpu
from jax.sharding import Mesh, PartitionSpec as P

AXES = ("chan", "zhi", "ring", "core", "space")
F32 = jnp.float32
BF16 = jnp.bfloat16
VMEM = pl.BlockSpec(memory_space=pltpu.VMEM)
SMEM = pl.BlockSpec(memory_space=pltpu.SMEM)


def permutation(sizes, move):
    pairs = []
    for source in range(math.prod(sizes)):
        target = move(*(int(v) for v in np.unravel_index(source, sizes)))
        if target is not None:
            pairs.append((source, int(np.ravel_multi_index(target, sizes))))
    return pairs


def neighbour(sizes, outer, turn):
    _, zhis, rings, cores, _ = sizes

    def move(chan, zhi, ring, core, space):
        column = (zhi * rings + ring) * cores + core
        if outer:
            column += 1 if column % 2 else -1
        if not 0 <= column < zhis * rings * cores:
            return None
        if turn:
            chan, space = space, chan
        return (chan, column // (rings * cores), column // cores % rings, column % cores, space)

    return permutation(sizes, move)


def height_mask(rows, height, at):
    return lax.broadcasted_iota(jnp.int32, (rows, 128), 0) % height == at


def shifted(value, height, step):
    rows = value.shape[0]
    edge = 0 if step < 0 else height - 1
    rolled = pltpu.roll(value, (-step) % rows, 0)
    return jnp.where(height_mask(rows, height, edge), 0.0, rolled)


def fill_padded(padded, pair, inner, core):
    planes, height, lanes = padded.shape[1:]
    planes -= 2
    zero = jnp.zeros((3, 1, height, lanes), BF16)
    padded[:, 0:1] = zero
    padded[:, planes + 1 : planes + 2] = zero
    for column, source in ((1, 0), (2 * core, 1)):
        if len(pair.shape) == 4:
            padded[column, 1 : planes + 1] = pair[source]
        else:
            slabs, _, depth = pair.shape[:3]
            for slab in range(slabs):
                padded[column, 1 + slab * depth : 1 + (slab + 1) * depth] = pair[slab, source]
    padded[2 - 2 * core, 1 : planes + 1] = inner[...]


def conv_kernel(backward, place, pair, inner, weight, *refs):
    *outs, padded, flat = refs
    slabs = len(outs)
    rows, lanes = outs[0].shape
    height = inner.shape[1]
    planes = rows // height
    fill_padded(padded, pair, inner, place[0])
    for cell in range(9):
        for r in range(3):
            if backward:
                flat[r * lanes : (r + 1) * lanes, cell * lanes : (cell + 1) * lanes] = weight[3 * cell + r]
            else:
                flat[cell * lanes : (cell + 1) * lanes, r * lanes : (r + 1) * lanes] = weight[3 * cell + r]
    for step, out in enumerate(outs):
        slab = lax.rem(place[1] + step, slabs)
        pieces = []
        for p in range(3):
            for q in range(3):
                column, plane = (2 - p, 2 - q) if backward else (p, q)
                start = slab * planes + plane
                pieces.append(padded[column, pl.ds(start, planes)].reshape(rows, lanes))
        lhs = jnp.concatenate(pieces, axis=1)
        dims = (((1,), (1 if backward else 0,)), ((), ()))
        taps = lax.dot_general(lhs, flat[...], dims, preferred_element_type=F32)
        low, high = (2, 0) if backward else (0, 2)
        total = taps[:, lanes : 2 * lanes]
        total += shifted(taps[:, low * lanes : (low + 1) * lanes], height, -1)
        total += shifted(taps[:, high * lanes : (high + 1) * lanes], height, 1)
        out[...] = total


def convolve(backward, core, me, pair, inner, weight, slabs):
    planes, height, lanes = inner.shape
    rows = planes * height
    flat = (3 * lanes, 9 * lanes) if backward else (9 * lanes, 3 * lanes)
    return pl.pallas_call(
        functools.partial(conv_kernel, backward),
        out_shape=[jax.ShapeDtypeStruct((rows // slabs, lanes), F32)] * slabs,
        in_specs=[SMEM, VMEM, VMEM, VMEM],
        out_specs=[VMEM] * slabs,
        scratch_shapes=[
            pltpu.VMEM((3, planes + 2, height, lanes), BF16),
            pltpu.VMEM(flat, BF16),
        ],
        compiler_params=pltpu.CompilerParams(vmem_limit_bytes=14 << 20),
        cost_estimate=pl.CostEstimate(
            flops=2 * 27 * rows * lanes * lanes, bytes_accessed=3 << 20, transcendentals=0
        ),
        name="input_grad" if backward else "forward",
    )(jnp.stack([core, me]), pair, inner, weight)


def filter_kernel(core, data, pair, inner, keep, send, own, padded, turned, taps):
    planes, height, lanes = inner.shape
    rows = planes * height
    fill_padded(padded, pair, inner, core[0])
    own[...] = data[:, 0].reshape(own.shape)
    flat = data[:, 0].reshape(rows, lanes).astype(F32)
    turned[0:lanes] = shifted(flat, height, -1).T.astype(BF16)
    turned[lanes : 2 * lanes] = flat.T.astype(BF16)
    turned[2 * lanes : 3 * lanes] = shifted(flat, height, 1).T.astype(BF16)
    for p in range(3):
        pieces = [padded[2 - p, 2 - q : 2 - q + planes].reshape(rows, lanes) for q in range(3)]
        rhs = jnp.concatenate(pieces, axis=1)
        result = jnp.dot(turned[...], rhs, preferred_element_type=F32)
        for q in range(3):
            for r in range(3):
                tap = 9 * p + 3 * q + r
                taps[tap * lanes : (tap + 1) * lanes] = result[
                    r * lanes : (r + 1) * lanes, q * lanes : (q + 1) * lanes
                ]
    taps[27 * lanes :] = jnp.zeros((lanes, lanes), F32)
    half = keep.shape[0]

    @pl.when(core[0] == 0)
    def _():
        keep[...] = taps[0:half]
        send[...] = taps[half : 2 * half]

    @pl.when(core[0] == 1)
    def _():
        keep[...] = taps[half : 2 * half]
        send[...] = taps[0:half]


def filter_partial(core, data, pair, inner):
    planes, height, lanes = inner.shape
    rows = planes * height
    half = jax.ShapeDtypeStruct((14 * lanes, lanes), F32)
    return pl.pallas_call(
        filter_kernel,
        out_shape=(half, half, jax.ShapeDtypeStruct(inner.shape, BF16)),
        in_specs=[SMEM, VMEM, VMEM, VMEM],
        out_specs=(VMEM, VMEM, VMEM),
        scratch_shapes=[
            pltpu.VMEM((3, planes + 2, height, lanes), BF16),
            pltpu.VMEM((3 * lanes, rows), BF16),
            pltpu.VMEM((28 * lanes, lanes), F32),
        ],
        compiler_params=pltpu.CompilerParams(vmem_limit_bytes=14 << 20),
        cost_estimate=pl.CostEstimate(
            flops=2 * 27 * rows * lanes * lanes, bytes_accessed=3 << 20, transcendentals=0
        ),
        name="filter_grad",
    )(core.reshape(1), data, pair, inner)


def small_call(kernel, shape, *operands):
    return pl.pallas_call(
        kernel,
        out_shape=jax.ShapeDtypeStruct(shape, F32),
        in_specs=[VMEM] * len(operands),
        out_specs=VMEM,
        compiler_params=pltpu.CompilerParams(vmem_limit_bytes=8 << 20),
        cost_estimate=pl.CostEstimate(
            flops=operands[0].size, bytes_accessed=1 << 20, transcendentals=0
        ),
    )(*operands)


def add_kernel(left, right, out):
    out[...] = left[...] + right[...]


def sum_kernel(parts, out):
    out[...] = (parts[0] + parts[1]) + (parts[2] + parts[3])


def spread_kernel(scale, left, right, out):
    total = (left[...] + right[...]) * scale
    for copy in range(out.shape[0]):
        out[copy] = total


def join_kernel(core, mine, other, out, sems):
    size, rest = mine.shape[0], out.shape[0] - mine.shape[0]

    def place(low, high):
        copies = [
            pltpu.make_async_copy(low, out.at[pl.ds(0, size)], sems.at[0]),
            pltpu.make_async_copy(high.at[pl.ds(0, rest)], out.at[pl.ds(size, rest)], sems.at[1]),
        ]
        for copy in copies:
            copy.start()
        for copy in copies:
            copy.wait()

    @pl.when(core[0] == 0)
    def _():
        place(mine, other)

    @pl.when(core[0] == 1)
    def _():
        place(other, mine)


def copy_kernel(block, out):
    out[...] = block[...]


def published(block):
    return pl.pallas_call(
        copy_kernel,
        out_shape=jax.ShapeDtypeStruct(block.shape, block.dtype),
        in_specs=[VMEM],
        out_specs=VMEM,
        compiler_params=pltpu.CompilerParams(vmem_limit_bytes=8 << 20),
        cost_estimate=pl.CostEstimate(flops=0, bytes_accessed=1 << 17, transcendentals=0),
        name="publish",
    )(block)


def pack_kernel(own, outer, out):
    for copy in range(out.shape[0]):
        out[copy, 0:1] = own[...]
        out[copy, 1:2] = outer[...]


def packed(own, outer, copies):
    return pl.pallas_call(
        pack_kernel,
        out_shape=jax.ShapeDtypeStruct((copies, 2, *own.shape[1:]), own.dtype),
        in_specs=[VMEM, VMEM],
        out_specs=VMEM,
        compiler_params=pltpu.CompilerParams(vmem_limit_bytes=8 << 20),
        cost_estimate=pl.CostEstimate(flops=0, bytes_accessed=1 << 19, transcendentals=0),
        name="pack",
    )(own, outer)


def joined(core, mine, other, shape):
    return pl.pallas_call(
        join_kernel,
        out_shape=jax.ShapeDtypeStruct(shape, F32),
        in_specs=[SMEM, VMEM, VMEM],
        out_specs=pl.BlockSpec(memory_space=pl.ANY),
        scratch_shapes=[pltpu.SemaphoreType.DMA((2,))],
        compiler_params=pltpu.CompilerParams(vmem_limit_bytes=8 << 20),
        cost_estimate=pl.CostEstimate(flops=0, bytes_accessed=4 << 20, transcendentals=0),
        name="join",
    )(core.reshape(1), mine, other)


def exchange(block, axis):
    return lax.all_to_all(block, axis, split_axis=0, concat_axis=0, tiled=True)


def rotate(term, axis, step):
    count = lax.axis_size(axis)
    return lax.ppermute(term, axis, [(i, (i + step) % count) for i in range(count)])


def doubling(step):
    return [
        (2 * zhi + core, 2 * (zhi ^ 1 if core == step else 3 - zhi) + core)
        for zhi in range(4)
        for core in range(2)
    ]


def after(value, *others):
    return lax.optimization_barrier((value, *others))[0]


def shards(sizes, activations, weight, output_grad):
    _, _, rings, cores, spaces = sizes
    planes, height, lanes = activations.shape[1:]
    core = lax.axis_index("core")
    swap = [(0, 1), (1, 0)]

    outer = lax.ppermute(activations, AXES, neighbour(sizes, True, False))
    grads = [lax.ppermute(output_grad, AXES, neighbour(sizes, far, True)) for far in (False, True)]
    grad = jnp.concatenate(grads, axis=0)
    grad, outer, own = lax.optimization_barrier((grad, outer, published(activations)))
    data = exchange(packed(own, outer, spaces), "space")
    grad = lax.all_gather(grad, "chan", axis=1, tiled=True)
    grad_inner = lax.ppermute(grad[0], "core", swap)

    keep, send, own = filter_partial(core, data, grad, grad_inner)
    moved = lax.ppermute(send, "core", swap)
    data_inner = lax.ppermute(after(own, send), "core", swap)
    half = small_call(add_kernel, keep.shape, keep, moved)
    half, data_inner = lax.optimization_barrier((half, data_inner))

    moved = exchange(half.reshape(rings, -1, lanes), "ring")
    me = lax.axis_index("space")
    back = convolve(True, core, me, after(grad, half), grad_inner, weight, spaces)
    back = [back[0], rotate(back[1], "space", 1), back[2], rotate(back[3], "space", 3)]
    quarter, *back = lax.optimization_barrier(
        (small_call(sum_kernel, moved.shape[1:], moved), *back)
    )

    moved = lax.ppermute(quarter, ("zhi", "core"), doubling(0))
    me = lax.axis_index("chan")
    forward = convolve(False, core, me, after(data, quarter), data_inner, weight, spaces)
    forward = [forward[0], rotate(forward[1], "chan", 1), rotate(forward[2], "chan", 2), forward[3]]
    cell_count = sizes[1] * rings * cores * grad.shape[1] * grad.shape[2]
    pair = quarter + moved
    pair, back, forward = lax.optimization_barrier((pair, back, forward))

    moved = lax.ppermute(pair, ("zhi", "core"), doubling(1))
    spread = functools.partial(spread_kernel, 1 / math.sqrt(cell_count))
    quarter = small_call(spread, (rings, *pair.shape), pair, moved)
    forward[3] = rotate(forward[3], "chan", 3)
    quarter, forward, back = lax.optimization_barrier((quarter, forward, back))

    half = exchange(quarter, "ring").reshape(-1, lanes)
    forward = sum(forward).astype(BF16).reshape(activations.shape)
    output = published(lax.ppermute(forward, AXES, neighbour(sizes, False, True)))
    back[2] = rotate(after(back[2], forward), "space", 2)
    half, _, back = lax.optimization_barrier((half, output, back))
    input_grad = sum(back).astype(BF16).reshape(activations.shape)

    other = lax.ppermute(half, "core", swap)
    blocks = (-1, *weight.shape[1:])
    filter_grad = joined(core, half.reshape(blocks), other.reshape(blocks), weight.shape)
    return output, input_grad, filter_grad


def solution(mesh):
    chans, filts, spaces = (mesh.shape[name] for name in ("chan", "filt", "space"))
    sizes = (chans, filts // 8, 4, 2, spaces)
    fine = Mesh(mesh.devices.reshape(sizes), AXES)
    cells = P(("zhi", "ring", "core"), "space", None, "chan")
    filters = P(None, "chan", "space")
    return jax.shard_map(
        functools.partial(shards, sizes),
        mesh=fine,
        in_specs=(cells, filters, cells),
        out_specs=(cells, cells, filters),
        check_vma=False,
    )
```
